32 devices in a mesh: groups: 2 (over y), row: 4 (over z), col: 2 (over x), sub: 2 (over core).
Axes of the slice: x: 2, y: 2, z: 4, core: 2. Of those that a mesh axis runs over, the one named last changes fastest.
Arguments:
- features: bfloat16 [1024, 512, 256], P(('groups', 'row', 'sub'), 'col'), parts along dimension 0, may hold values from -96 to 96
- seeds: int32 [1024, 512], P(('groups', 'row', 'sub'), 'col'), parts along dimension 0, may hold values from 0 to 64, as said below
- valid_tiles: int32 [8, 2], P(('groups', 'row'), 'col'), parts along dimension 0, may hold values from 0 to 1, as said below
- prototypes: bfloat16 [128, 4, 256], P('groups'), parts along dimension 0, may hold values from -1 to 1
Outputs:
- refined_protos: float32 [128, 4, 256], P('groups'), parts along dimension 0
- beliefs: float32 [128, 512, 512], P('groups', ('row', 'sub'), 'col'), parts along dimension 0
The draws below stay inside these ranges and needn't reach their ends.
There are 2 independent parts, one for each index of `groups`. The reference program is written for one: setup_inputs(seed, part) draws one part's arguments, and reference() takes and returns one part's arrays. A program takes and returns all parts, laid end to end along the dimension named above; each array names one. Nothing has to cross between parts.
Inputs may be any that keep to these rules, and one draw needn't show every extreme that they name: seeds[h, w] is a token's seed class, or 64 for a token without a seed. `valid_tiles`: every region has at least one masked and at least one usable tile.
All inputs are finite; a program needn't handle non-finite values.
Results may differ from the reference program's by a relative error of at most 0.0066.
Values sent between devices are 32-bit elements; how exact they have to be, the bound alone decides.
No kernel may reach another device: no remote copies, remote signals or barrier semaphores. Data moves between devices by JAX's collectives and lax.ppermute only.
A program may use at most 128 MiB of HBM per device.

```python
import math
import jax
import jax.numpy as jnp
from jax import lax

C = 256
K = 64
M = 4
TH = 64
TW = 256
ITERS = 2
NH = 512
NW = 512
N_ROW = 4
N_COL = 2
N_SUB = 2


def draw_class_labels(key):
    return jax.random.randint(jax.random.fold_in(key, 13), (NH, NW), 0, K + 1).astype(jnp.int32)


def draw_protos(key):
    base = jax.random.truncated_normal(jax.random.fold_in(key, 11), -3.0, 3.0, (K, M, C), jnp.float32)
    return base / math.sqrt(C)


def draw_seeds(key, part):
    return draw_class_labels(key)


def draw_prototypes(key, part):
    return draw_protos(key).astype(jnp.bfloat16)


def draw_valid_tiles(key, part):
    count = N_ROW * N_COL
    base = jax.random.randint(jax.random.fold_in(key, 31), (count,), 0, 4).astype(jnp.int32)
    zero_at = jax.random.randint(jax.random.fold_in(key, 32), (), 0, count).astype(jnp.int32)
    step_on = jax.random.randint(jax.random.fold_in(key, 33), (), 0, count - 1).astype(jnp.int32)
    one_at = (zero_at + 1 + step_on) % count
    places = jnp.arange(count, dtype=jnp.int32)
    flags = jnp.where(base > 0, 1, 0).astype(jnp.int32)
    flags = jnp.where(places == zero_at, 0, flags)
    flags = jnp.where(places == one_at, 1, flags)
    return flags.reshape(N_ROW, N_COL).astype(jnp.int32)


def draw_features(key, part):
    values = jax.random.truncated_normal(jax.random.fold_in(key, 12), -4.5, 4.5, (NH, NW, C), jnp.float32)
    return jnp.clip(values, -96.0, 96.0).astype(jnp.bfloat16)


def setup_inputs(seed: int = 0, part: int = 0) -> dict:
    keys = jax.random.split(jax.random.key(seed), 5)
    own_keys = jax.random.split(jax.random.fold_in(keys[4], part), 5)
    features = draw_features(jax.random.fold_in(jax.random.fold_in(keys[4], part), 71), part)
    seeds = draw_seeds(jax.random.fold_in(jax.random.fold_in(keys[4], part), 71), part)
    valid_tiles = draw_valid_tiles(jax.random.fold_in(jax.random.fold_in(keys[4], part), 71), part)
    prototypes = draw_prototypes(jax.random.fold_in(jax.random.fold_in(keys[4], part), 71), part)
    return {"features": features, "seeds": seeds, "valid_tiles": valid_tiles, "prototypes": prototypes}


SCALE = 2.0
SEED_REWARD = 2.0
PAIR = 1.0
LOW = -1e+30

def tile_valid(valid_tiles):
    spread = jnp.repeat(valid_tiles, TH * N_SUB, axis=0)
    return jnp.repeat(spread, TW, axis=1).astype(jnp.float32)

def gather_taps(padded, height, breadth):
    refined_output = jnp.zeros((padded.shape[0], height, breadth), jnp.float32)
    for shift_y in range(-3, 4):
        for shift_x in range(-3, 4):
            if shift_y == 0 and shift_x == 0:
                continue
            factor = math.exp(-(shift_y * shift_y + shift_x * shift_x) / 8.0)
            refined_output = refined_output + factor * padded[:, 3 + shift_y:3 + shift_y + height, 3 + shift_x:3 + shift_x + breadth]
    return refined_output

def reference(features, seeds, valid_tiles, prototypes):
    block = TH * N_SUB
    valid = tile_valid(valid_tiles)
    feat_blocks = features.reshape(N_ROW, block, NW, C)
    seed_blocks = seeds.reshape(N_ROW, block, NW)
    valid_blocks = valid.reshape(N_ROW, block, NW)
    class_labels = jnp.arange(K, dtype=jnp.int32)[:, None, None]
    protos32 = prototypes.astype(jnp.float32)

    def scores_of(feat_block):
        return SCALE * jnp.einsum('kmc,hwc->kmhw', protos32, feat_block.astype(jnp.float32))

    def member_of(seed_tile_block, valid_block):
        return (seed_tile_block[None] == class_labels) & (valid_block[None] > 0.5)

    def peak_of(items):
        feat_block, seed_tile_block, valid_block = items
        score = scores_of(feat_block)
        member = member_of(seed_tile_block, valid_block)
        return lax.optimization_barrier(jnp.max(jnp.where(member[:, None], score, LOW), axis=(2, 3)))
    peak = lax.optimization_barrier(jnp.max(lax.map(peak_of, (feat_blocks, seed_blocks, valid_blocks)), axis=0))

    def sums_of(items):
        feat_block, seed_tile_block, valid_block = items
        score = scores_of(feat_block)
        member = member_of(seed_tile_block, valid_block)
        masked = jnp.where(member[:, None], score, LOW)
        weights = jnp.where(member[:, None], jnp.exp(masked - peak[:, :, None, None]), 0.0)
        block_total = lax.optimization_barrier(jnp.sum(weights, axis=(2, 3)))
        rounded = weights.astype(jnp.bfloat16).astype(jnp.float32)
        block_sum = jnp.einsum('kmhw,hwc->kmc', rounded, feat_block.astype(jnp.float32))
        return (block_total, block_sum)
    totals, sums = lax.map(sums_of, (feat_blocks, seed_blocks, valid_blocks))
    total = lax.optimization_barrier(jnp.sum(totals, axis=0))
    pooled = lax.optimization_barrier(jnp.sum(sums, axis=0)) / total[:, :, None]
    refined = pooled / jnp.sqrt(lax.optimization_barrier(jnp.sum(pooled * pooled, axis=2, keepdims=True)) + 1e-06)
    refined32 = refined.astype(jnp.bfloat16).astype(jnp.float32)

    def unary_of(items):
        feat_block, seed_tile_block = items
        second_pass = SCALE * jnp.einsum('kmc,hwc->kmhw', refined32, feat_block.astype(jnp.float32))
        seed_reward = SEED_REWARD * (seed_tile_block[None] == class_labels).astype(jnp.float32)
        return jax.nn.logsumexp(second_pass, axis=1) + seed_reward
    unary_potential = lax.map(unary_of, (feat_blocks, seed_blocks))
    unary_potential = jnp.transpose(unary_potential, (1, 0, 2, 3)).reshape(K, NH, NW)
    belief = jax.nn.softmax(unary_potential, axis=0) * valid[None]
    for step in range(ITERS):
        padded = jnp.pad(belief, ((0, 0), (3, 3), (3, 3)))
        message = gather_taps(padded, NH, NW)
        belief = jax.nn.softmax(unary_potential + PAIR * message, axis=0) * valid[None]
    return (refined, belief)
```

```python
import functools
import math

import jax
import jax.numpy as jnp
import numpy as np
from jax import lax
from jax.experimental import pallas as pl
from jax.experimental.pallas import tpu as pltpu
from jax.sharding import PartitionSpec as P

ITERS = 2
SCALE = 2.0
SEED_REWARD = 2.0
LOW = -1e30
REACH = 3
HALO = ITERS * REACH
LANES = 128
STATS = 8
PACK = 16
GAIN = 1.461325
TAPS = [math.exp(-(d * d) / 8.0) / GAIN for d in range(REACH + 1)]
F32 = jnp.float32
BF16 = jnp.bfloat16


def cost(flops, moved):
    return pl.CostEstimate(flops=flops, bytes_accessed=moved, transcendentals=0)


def across_taps(cols):
    place = np.full(cols + LANES, -(10**6))
    place[:cols] = np.arange(cols)
    place[cols : cols + HALO] = np.arange(-HALO, 0)
    place[cols + HALO : cols + 2 * HALO] = np.arange(cols, cols + HALO)
    gap = np.abs(place[:, None] - place[None, :])
    used = (place[:, None] > -(10**5)) & (place[None, :] > -(10**5)) & (gap <= REACH)
    return np.where(used, GAIN * np.exp(-np.minimum(gap, REACH) ** 2 / 8.0), 0.0)


def pool_kernel(meta, seeds, feats, protos, keep, give, score, weight, acc, peak, total):
    rows, cols, chans = feats.shape
    count = protos.shape[0]
    classes = count // 4
    step = pl.program_id(0)

    @pl.when(step == 0)
    def _():
        acc[...] = jnp.zeros_like(acc)
        total[...] = jnp.zeros_like(total)
        peak[...] = jnp.full_like(peak, LOW)

    labels = lax.broadcasted_iota(jnp.int32, (classes, cols), 0)
    top = jnp.full((count, LANES), LOW, F32)
    for r in range(rows):
        here = jnp.where(meta[0] > 0, seeds[r : r + 1, :], -1)
        member = here == labels
        raw = lax.dot_general(
            protos[...], feats[r], (((1,), (1,)), ((), ())), preferred_element_type=F32
        )
        masked = jnp.concatenate(
            [
                jnp.where(member, raw[m * classes : (m + 1) * classes], LOW)
                for m in range(count // classes)
            ],
            axis=0,
        )
        score[:, r * cols : (r + 1) * cols] = masked
        for c in range(cols // LANES):
            top = jnp.maximum(top, masked[:, c * LANES : (c + 1) * LANES])
    before = peak[...]
    after = jnp.maximum(before, jnp.max(top, axis=1, keepdims=True))
    fade = jnp.exp(before - after)
    shift = jnp.maximum(after, 0.1 * LOW)
    gained = jnp.zeros((count, LANES), F32)
    for c in range(rows * cols // LANES):
        part = jnp.exp(score[:, c * LANES : (c + 1) * LANES] - shift)
        gained = gained + part
        weight[:, c * LANES : (c + 1) * LANES] = part.astype(BF16)
    peak[...] = after
    total[...] = total[...] * fade + gained
    flat = feats[...].reshape(rows * cols, chans)
    acc[...] = acc[...] * fade[:, :1] + jnp.dot(weight[...], flat, preferred_element_type=F32)

    @pl.when(step == pl.num_programs(0) - 1)
    def _():
        sub = meta[1]
        sums = acc[...].T
        tops = peak[...].T[:1]
        totals = jnp.sum(total[...].T, axis=0, keepdims=True)
        half = count // 2

        def write(ref, second):
            lanes = slice(half, count) if second else slice(0, half)
            ref[:chans, :] = sums[:, lanes]
            ref[chans : chans + 1, :] = tops[:, lanes]
            ref[chans + 1 : chans + 2, :] = totals[:, lanes]
            ref[chans + 2 :, :] = jnp.zeros((STATS - 2, half), F32)

        @pl.when(sub == 0)
        def _():
            write(keep, False)
            write(give, True)

        @pl.when(sub != 0)
        def _():
            write(keep, True)
            write(give, False)


def pool(meta, seeds, feats, protos):
    height, cols, chans = feats.shape
    count = protos.shape[0]
    rows = 8
    piece = jax.ShapeDtypeStruct((chans + STATS, count // 2), F32)
    whole = pl.BlockSpec((chans + STATS, count // 2), lambda i, *_: (0, 0))
    return pl.pallas_call(
        pool_kernel,
        out_shape=(piece, piece),
        grid_spec=pltpu.PrefetchScalarGridSpec(
            num_scalar_prefetch=1,
            grid=(height // rows,),
            in_specs=[
                pl.BlockSpec((rows, cols), lambda i, *_: (i, 0)),
                pl.BlockSpec((rows, cols, chans), lambda i, *_: (i, 0, 0)),
                pl.BlockSpec((count, chans), lambda i, *_: (0, 0)),
            ],
            out_specs=(whole, whole),
            scratch_shapes=[
                pltpu.VMEM((count, rows * cols), F32),
                pltpu.VMEM((count, rows * cols), BF16),
                pltpu.VMEM((count, chans), F32),
                pltpu.VMEM((count, LANES), F32),
                pltpu.VMEM((count, LANES), F32),
            ],
        ),
        compiler_params=pltpu.CompilerParams(vmem_limit_bytes=24 << 20),
        cost_estimate=cost(4 * height * cols * chans * count, height * cols * chans * 2),
        name="pool",
    )(meta, seeds, feats, protos)


def merge_kernel(a, b, out):
    chans = a.shape[0] - STATS
    at, bt = a[chans : chans + 1, :], b[chans : chans + 1, :]
    top = jnp.maximum(at, bt)
    fa, fb = jnp.exp(at - top), jnp.exp(bt - top)
    out[:chans, :] = a[:chans, :] * fa + b[:chans, :] * fb
    out[chans : chans + 1, :] = top
    out[chans + 1 : chans + 2, :] = (
        a[chans + 1 : chans + 2, :] * fa + b[chans + 1 : chans + 2, :] * fb
    )
    out[chans + 2 :, :] = jnp.zeros((STATS - 2, a.shape[1]), F32)


def merge(a, b):
    return pl.pallas_call(
        merge_kernel,
        out_shape=jax.ShapeDtypeStruct(a.shape, F32),
        in_specs=[pl.BlockSpec(memory_space=pltpu.VMEM)] * 2,
        out_specs=pl.BlockSpec(memory_space=pltpu.VMEM),
        cost_estimate=cost(3 * a.size, 12 * a.size),
        name="merge",
    )(a, b)


def field_kernel(
    meta, keep, got, near, far, codes, strip, strip_codes, taps, feats,
    refined, out,
    held, base, belief, second, lhs, sums, mixed, result, sem, out_sem,
):
    height, cols, chans = feats.shape
    count = sums.shape[1]
    classes = count // 4
    wide = cols + LANES
    sub = meta[1]
    groups = 8

    def fetch(i):
        rows = height // groups
        return pltpu.make_async_copy(
            feats.at[pl.ds(i * rows, rows)], held.at[pl.ds(i * rows, rows)], sem.at[i]
        )

    for i in range(groups):
        fetch(i).start()

    half = count // 2
    first = pl.multiple_of(sub * half, half)
    other = pl.multiple_of((1 - sub) * half, half)
    sums[:, pl.ds(first, half)] = keep[...]
    sums[:, pl.ds(other, half)] = got[...]
    pooled = sums[:chans, :] / sums[chans + 1 : chans + 2, :]
    length = jnp.sqrt(jnp.sum(pooled * pooled, axis=0, keepdims=True) + 1e-06)
    ready = (pooled / length).T
    for c in range(chans // LANES):
        lanes = slice(c * LANES, (c + 1) * LANES)
        for m in range(4):
            mixed[c, pl.ds(m, classes, stride=4), :] = ready[m * classes : (m + 1) * classes, lanes]
        refined[:, lanes] = mixed[c]
    lead = (ready.astype(BF16).astype(F32) * SCALE).astype(BF16)

    labels = lax.broadcasted_iota(jnp.int32, (classes, 1), 0) + 1
    bonus = math.exp(SEED_REWARD)

    def unary(tokens, code):
        raw = lax.dot_general(lead, tokens, (((1,), (1,)), ((), ())), preferred_element_type=F32)
        parts = [raw[m * classes : (m + 1) * classes] for m in range(4)]
        top = functools.reduce(jnp.maximum, parts)
        top = jnp.max(top, axis=0, keepdims=True)
        top = jnp.where(code == 0, 1e30, top)
        grown = functools.reduce(jnp.add, [jnp.exp(part - top) for part in parts])
        grown = jnp.where(labels == code, grown * bonus, grown)
        return grown, share(grown)

    def share(grown):
        norm = jnp.sum(grown, axis=0, keepdims=True)
        return grown * (1.0 / jnp.maximum(norm, 1e-30))

    def edge(ref, i, row):
        tokens = ref[pl.ds(pl.multiple_of(i * cols, cols), cols), :].astype(BF16)
        code = ref[pl.ds(HALO * cols + i, 1), :].astype(jnp.int32)
        grown, first_belief = unary(tokens, code)
        base[row, :, :cols] = grown
        belief[row, :, :cols] = first_belief

    near_at = jnp.where(sub == 0, HALO + height, 0)
    far_at = jnp.where(sub == 0, 0, HALO + height)

    @pl.loop(0, HALO)
    def _(i):
        edge(near, i, near_at + i)
        edge(far, i, far_at + i)

    for g in range(strip.shape[0]):
        grown, first_belief = unary(strip[g], strip_codes[g : g + 1, :])
        for r in range(LANES // PACK):
            row = g * (LANES // PACK) + r
            if row < height + 2 * HALO:
                turn = (LANES - r * PACK) % LANES
                base[row, :, cols:] = pltpu.roll(grown, turn, 1) if turn else grown
                belief[row, :, cols:] = pltpu.roll(first_belief, turn, 1) if turn else first_belief

    for i in range(groups):
        fetch(i).wait()
        rows = height // groups

        @pl.loop(0, rows)
        def _(j):
            row = i * rows + j
            grown, first_belief = unary(held[row], codes[pl.ds(row, 1), :])
            base[HALO + row, :, :cols] = grown
            belief[HALO + row, :, :cols] = first_belief

    def mix(source, row, slot):
        centre = source[row]
        tall = TAPS[0] * centre
        for d in range(1, REACH + 1):
            tall = tall + TAPS[d] * (source[row - d] + source[row + d])
        high = tall.astype(BF16)
        low = (tall - high.astype(F32)).astype(BF16)
        at = pl.ds(slot * classes, classes)
        lhs[at, :cols] = high[:, :cols]
        lhs[at, cols : 2 * cols] = low[:, :cols]
        lhs[at, 2 * cols : 2 * cols + LANES] = high[:, cols:]
        lhs[at, 2 * cols + LANES :] = low[:, cols:]

    batch = 7

    @pl.loop(0, (height + 2 * REACH) // batch)
    def _(i):
        start = REACH + i * batch
        for j in range(batch):
            mix(belief, start + j, j)
        message = jnp.dot(lhs[: batch * classes, :], taps[...], preferred_element_type=F32)
        for j in range(batch):
            row = start + j
            sent = message[j * classes : (j + 1) * classes, :] - belief[row]
            second[row] = share(base[row] * jnp.exp(sent))

    batch = 8
    tiles = cols // LANES
    flat = result.reshape(tiles * classes * height, LANES)

    def leave(i, c):
        rows = pl.ds(pl.multiple_of(i * batch, batch), batch)
        return pltpu.make_async_copy(
            result.at[c, :, rows, :],
            out.at[:, rows, pl.ds(c * LANES, LANES)],
            out_sem.at[i, c],
        )

    @pl.loop(0, height // batch)
    def _(i):
        start = HALO + i * batch
        for j in range(batch):
            mix(second, start + j, j)
        message = jnp.dot(
            lhs[: batch * classes, :], taps[:, :cols], preferred_element_type=F32
        )
        for j in range(batch):
            row = start + j
            sent = message[j * classes : (j + 1) * classes, :] - second[row, :, :cols]
            done = share(base[row, :, :cols] * jnp.exp(sent))
            for c in range(tiles):
                at = c * classes * height + row - HALO
                flat[pl.ds(at, classes, stride=height), :] = done[:, c * LANES : (c + 1) * LANES]
        for c in range(tiles):
            leave(i, c).start()

    @pl.loop(0, height // batch)
    def _(i):
        for c in range(tiles):
            leave(i, c).wait()


def field(meta, keep, got, near, far, codes, strip, strip_codes, feats, count):
    height, cols, chans = feats.shape
    classes = count // 4
    wide = cols + LANES
    deep = height + 2 * HALO
    across = across_taps(cols)
    taps = np.concatenate([across[:cols], across[:cols], across[cols:], across[cols:]], axis=0)
    vmem = pl.BlockSpec(memory_space=pltpu.VMEM)
    return pl.pallas_call(
        field_kernel,
        out_shape=(
            jax.ShapeDtypeStruct((count, chans), F32),
            jax.ShapeDtypeStruct((classes, height, cols), F32),
        ),
        in_specs=[pl.BlockSpec(memory_space=pltpu.SMEM)]
        + [vmem] * 8
        + [pl.BlockSpec(memory_space=pl.ANY)],
        out_specs=(vmem, pl.BlockSpec(memory_space=pl.ANY)),
        scratch_shapes=[
            pltpu.VMEM((height, cols, chans), BF16),
            pltpu.VMEM((deep, classes, wide), F32),
            pltpu.VMEM((deep, classes, wide), F32),
            pltpu.VMEM((deep, classes, wide), F32),
            pltpu.VMEM((8 * classes, 2 * wide), BF16),
            pltpu.VMEM((chans + STATS, count), F32),
            pltpu.VMEM((chans // LANES, count, LANES), F32),
            pltpu.VMEM((cols // LANES, classes, height, LANES), F32),
            pltpu.SemaphoreType.DMA((8,)),
            pltpu.SemaphoreType.DMA((height // 8, cols // LANES)),
        ],
        compiler_params=pltpu.CompilerParams(vmem_limit_bytes=56 << 20),
        cost_estimate=cost(8 * height * cols * chans * count, 16 << 20),
        name="field",
    )(meta, keep, got, near, far, codes, strip, strip_codes, jnp.asarray(taps, BF16), feats)


def swap(x, axes, pairs):
    return lax.ppermute(x, axes, [p for a, b in pairs for p in ((a, b), (b, a))])


def on_device(features, seeds, valid_tiles, prototypes):
    height, cols, chans = features.shape
    classes, modes, _ = prototypes.shape
    count = classes * modes
    n_row, n_col = lax.axis_size("row"), lax.axis_size("col")
    sub, col = lax.axis_index("sub"), lax.axis_index("col")
    meta = jnp.stack([valid_tiles[0, 0], sub]).astype(jnp.int32)
    codes = jnp.where(valid_tiles[0, 0] > 0, seeds + 1, 0)
    protos = (SCALE * prototypes.astype(F32)).astype(BF16)
    protos = protos.transpose(1, 0, 2).reshape(count, chans)

    def edge_rows(start):
        rows = lax.dynamic_slice_in_dim(features, start, HALO, axis=0).astype(F32)
        marks = lax.dynamic_slice_in_dim(codes, start, HALO, axis=0).astype(F32)
        return jnp.concatenate([rows.reshape(-1, chans), marks.reshape(-1, chans)], axis=0)

    low_edge = height - HALO
    near = swap(edge_rows(jnp.where(sub == 0, low_edge, 0)), "sub", [(0, 1)])
    far = swap(
        edge_rows(jnp.where(sub == 0, 0, low_edge)),
        ("row", "sub"),
        [(2 * i + 1, 2 * i + 2) for i in range(n_row - 1)],
    )

    keep, give = pool(meta, seeds, features, protos)
    keep = merge(keep, swap(give, "sub", [(0, 1)]))
    stride = 1
    while stride < n_col:
        pairs = [(i, i | stride) for i in range(n_col) if not i & stride]
        keep = merge(keep, swap(keep, "col", pairs))
        stride *= 2
    stride = 1
    while stride < n_row:
        pairs = [(i, i | stride) for i in range(n_row) if not i & stride]
        keep = merge(keep, swap(keep, "row", pairs))
        stride *= 2
        if stride == 2:
            keep, near, far = lax.optimization_barrier((keep, near, far))

            def edge_cols(start):
                def cut(msg):
                    rows = msg[: HALO * cols].reshape(HALO, cols, chans)
                    marks = msg[HALO * cols :].reshape(HALO, cols)
                    return (
                        lax.dynamic_slice_in_dim(rows, start, HALO, axis=1),
                        lax.dynamic_slice_in_dim(marks, start, HALO, axis=1),
                    )

                near_part, far_part = cut(near), cut(far)
                mine = (
                    lax.dynamic_slice_in_dim(features, start, HALO, axis=1).astype(F32),
                    lax.dynamic_slice_in_dim(codes, start, HALO, axis=1).astype(F32),
                )
                rows, marks = (
                    jnp.concatenate(
                        [
                            jnp.where(sub == 0, f, n),
                            o,
                            jnp.where(sub == 0, n, f),
                        ],
                        axis=0,
                    )
                    for n, o, f in zip(near_part, mine, far_part)
                )
                rows = rows.reshape(-1, chans)
                marks = marks.reshape(-1)
                marks = jnp.pad(marks, (0, -marks.shape[0] % chans)).reshape(-1, chans)
                return jnp.concatenate([rows, marks], axis=0)

            even = col % 2 == 0
            right_edge = cols - HALO
            one = swap(
                edge_cols(jnp.where(even, right_edge, 0)),
                "col",
                [(i, i + 1) for i in range(0, n_col - 1, 2)],
            )
            if n_col > 2:
                two = swap(
                    edge_cols(jnp.where(even, 0, right_edge)),
                    "col",
                    [(i, i + 1) for i in range(1, n_col - 1, 2)],
                )
            else:
                two = jnp.zeros_like(one)
    got = swap(keep, "sub", [(0, 1)])

    deep = height + 2 * HALO
    left = jnp.where(even, two, one)
    right = jnp.where(even, one, two)

    def unpack(msg):
        rows = msg[: deep * HALO].reshape(deep, HALO, chans)
        marks = msg[deep * HALO :].reshape(-1)[: deep * HALO].reshape(deep, HALO)
        return rows, marks

    (left_rows, left_marks), (right_rows, right_marks) = unpack(left), unpack(right)
    per = LANES // PACK
    more = (-deep % per, PACK - 2 * HALO)
    strip = jnp.concatenate([left_rows, right_rows], axis=1).astype(BF16)
    strip = jnp.pad(strip, ((0, more[0]), (0, more[1]), (0, 0))).reshape(-1, LANES, chans)
    marks = jnp.concatenate([left_marks, right_marks], axis=1).astype(jnp.int32)
    marks = jnp.pad(marks, ((0, more[0]), (0, more[1]))).reshape(-1, LANES)

    refined, belief = field(meta, keep, got, near, far, codes, strip, marks, features, count)
    return refined.reshape(classes, modes, chans), belief


def solution(mesh):
    placed = (
        P(("groups", "row", "sub"), "col", None),
        P(("groups", "row", "sub"), "col"),
        P(("groups", "row"), "col"),
        P("groups", None, None),
    )
    return jax.shard_map(
        on_device,
        mesh=mesh,
        in_specs=placed,
        out_specs=(P("groups", None, None), P("groups", ("row", "sub"), "col")),
        check_vma=False,
    )
```

```python
import functools
import math

import jax
import jax.numpy as jnp
import numpy as np
from jax import lax
from jax.experimental import pallas as pl
from jax.experimental.pallas import tpu as pltpu
from jax.sharding import PartitionSpec as P

ITERS = 2
SCALE = 2.0
SEED_REWARD = 2.0
LOW = -1e30
REACH = 3
HALO = ITERS * REACH
LANES = 128
STATS = 8
SIDE = 8
GAIN = 1.461325
TAPS = [math.exp(-(d * d) / 8.0) / GAIN for d in range(REACH + 1)]
F32 = jnp.float32
BF16 = jnp.bfloat16
VMEM = pl.BlockSpec(memory_space=pltpu.VMEM)
SMEM = pl.BlockSpec(memory_space=pltpu.SMEM)
ANY = pl.BlockSpec(memory_space=pl.ANY)


def cost(flops, moved):
    return pl.CostEstimate(flops=flops, bytes_accessed=moved, transcendentals=0)


def params(mib):
    return pltpu.CompilerParams(vmem_limit_bytes=mib << 20)


def across_taps(cols, sides):
    both = []
    for odd in (False, True):
        place = np.full(cols + LANES, -(10**6))
        place[:cols] = np.arange(cols)
        right, left = (cols + SIDE, cols) if odd else (cols, cols + SIDE)
        if sides == 2 or not odd:
            place[right : right + HALO] = cols + np.arange(HALO)
        if sides == 2 or odd:
            place[left + SIDE - HALO : left + SIDE] = np.arange(-HALO, 0)
        gap = np.abs(place[:, None] - place[None, :])
        used = (place[:, None] > -(10**5)) & (place[None, :] > -(10**5)) & (gap <= REACH)
        taps = np.where(used, GAIN * np.exp(-np.minimum(gap, REACH) ** 2 / 8.0), 0.0)
        both.append(np.concatenate([taps[:cols], taps[:cols], taps[cols:], taps[cols:]], axis=0))
    return np.stack(both)


def ends_kernel(meta, seeds, feats, near, far, held, sem):
    height, cols, chans = feats.shape
    fetch = [
        pltpu.make_async_copy(feats.at[pl.ds(at, HALO)], held.at[i], sem.at[i])
        for i, at in enumerate((0, height - HALO))
    ]
    for copy in fetch:
        copy.start()
    for copy in fetch:
        copy.wait()

    def write(ref, i):
        at = (0, height - HALO)[i]
        for r in range(HALO):
            ref[r * cols : (r + 1) * cols, :] = held[i, r].astype(F32)
        marks = jnp.where(meta[0] > 0, seeds[at : at + HALO, :] + 1, 0)
        ref[HALO * cols :, :] = marks.astype(F32)

    @pl.when(meta[1] == 0)
    def _():
        write(near, 1)
        write(far, 0)

    @pl.when(meta[1] != 0)
    def _():
        write(near, 0)
        write(far, 1)


def ends(meta, seeds, feats):
    height, cols, chans = feats.shape
    message = jax.ShapeDtypeStruct((HALO * cols + HALO, chans), F32)
    return pl.pallas_call(
        ends_kernel,
        out_shape=(message, message),
        in_specs=[SMEM, VMEM, ANY],
        out_specs=(VMEM, VMEM),
        scratch_shapes=[
            pltpu.VMEM((2, HALO, cols, chans), BF16),
            pltpu.SemaphoreType.DMA((2,)),
        ],
        compiler_params=params(8),
        cost_estimate=cost(0, 4 << 20),
        name="ends",
    )(meta, seeds, feats)


def side_kernel(meta, seeds, near, far, feats, out, held, marks, sem):
    height, cols, chans = feats.shape
    deep = marks.shape[0]
    width = held.shape[1]
    sub, left = meta[1], meta[2]
    start = pl.multiple_of(jnp.where(left > 0, 0, cols - width), width)
    copy = pltpu.make_async_copy(feats.at[:, pl.ds(start, width), :], held, sem)
    copy.start()
    marks[...] = jnp.zeros_like(marks)
    marks[HALO : HALO + height, :] = jnp.where(meta[0] > 0, seeds[...] + 1, 0).astype(F32)
    low, skip = HALO + height, jnp.where(left > 0, 0, cols - SIDE)
    skip = pl.multiple_of(skip, SIDE)

    def ends_of(ref, at):
        marks[at : at + HALO, :] = ref[HALO * cols :, :]
        for r in range(HALO):
            out[(at + r) * SIDE : (at + r + 1) * SIDE, :] = ref[pl.ds(r * cols + skip, SIDE), :]

    @pl.when(sub == 0)
    def _():
        ends_of(near, low)
        ends_of(far, 0)

    @pl.when(sub != 0)
    def _():
        ends_of(far, low)
        ends_of(near, 0)

    lane = lax.broadcasted_iota(jnp.int32, (cols, LANES), 1)
    source = lax.broadcasted_iota(jnp.int32, (cols, LANES), 0)
    spread = (source == lane % SIDE + skip).astype(BF16)
    spun = jnp.dot(marks[...].astype(BF16), spread, preferred_element_type=F32)
    per = LANES // SIDE
    groups = deep // per
    mine = lax.broadcasted_iota(jnp.int32, (per, LANES), 1) // SIDE
    mine = mine == lax.broadcasted_iota(jnp.int32, (per, LANES), 0)
    out[deep * SIDE :, :] = jnp.zeros((STATS, chans), F32)
    for g in range(groups):
        row = jnp.where(mine, spun[g * per : (g + 1) * per], 0.0)
        out[deep * SIDE + g : deep * SIDE + g + 1, :LANES] = jnp.sum(row, axis=0, keepdims=True)
    out[(height + 2 * HALO) * SIDE : deep * SIDE, :] = jnp.zeros(
        ((deep - height - 2 * HALO) * SIDE, chans), F32
    )
    copy.wait()

    @pl.when(left > 0)
    def _():
        for r in range(height):
            at = (HALO + r) * SIDE
            out[at : at + SIDE, :] = held[r].astype(F32)[:SIDE]

    @pl.when(left == 0)
    def _():
        for r in range(height):
            at = (HALO + r) * SIDE
            out[at : at + SIDE, :] = held[r].astype(F32)[width - SIDE :]


def side(meta, seeds, near, far, feats):
    height, cols, chans = feats.shape
    per = LANES // SIDE
    deep = -(-(height + 2 * HALO) // per) * per
    return pl.pallas_call(
        side_kernel,
        out_shape=jax.ShapeDtypeStruct((deep * SIDE + STATS, chans), F32),
        in_specs=[SMEM, VMEM, VMEM, VMEM, ANY],
        out_specs=VMEM,
        scratch_shapes=[
            pltpu.VMEM((height, 2 * SIDE, chans), BF16),
            pltpu.VMEM((deep, cols), F32),
            pltpu.SemaphoreType.DMA(()),
        ],
        compiler_params=params(8),
        cost_estimate=cost(0, 2 << 20),
        name="side",
    )(meta, seeds, near, far, feats)


def pool_kernel(meta, seeds, feats, protos, keep, give, score, weight, acc, peak, total):
    rows, cols, chans = feats.shape
    count = protos.shape[0]
    classes = count // 4
    step = pl.program_id(0)

    @pl.when(step == 0)
    def _():
        acc[...] = jnp.zeros_like(acc)
        total[...] = jnp.zeros_like(total)
        peak[...] = jnp.full_like(peak, LOW)

    labels = lax.broadcasted_iota(jnp.int32, (classes, cols), 0)
    top = jnp.full((count, LANES), LOW, F32)
    for r in range(rows):
        here = jnp.where(meta[0] > 0, seeds[r : r + 1, :], -1)
        member = here == labels
        raw = lax.dot_general(
            protos[...], feats[r], (((1,), (1,)), ((), ())), preferred_element_type=F32
        )
        masked = jnp.concatenate(
            [
                jnp.where(member, raw[m * classes : (m + 1) * classes], LOW)
                for m in range(count // classes)
            ],
            axis=0,
        )
        score[:, r * cols : (r + 1) * cols] = masked
        for c in range(cols // LANES):
            top = jnp.maximum(top, masked[:, c * LANES : (c + 1) * LANES])
    before = peak[...]
    after = jnp.maximum(before, jnp.max(top, axis=1, keepdims=True))
    fade = jnp.exp(before - after)
    shift = jnp.maximum(after, 0.1 * LOW)
    gained = jnp.zeros((count, LANES), F32)
    for c in range(rows * cols // LANES):
        part = jnp.exp(score[:, c * LANES : (c + 1) * LANES] - shift)
        gained = gained + part
        weight[:, c * LANES : (c + 1) * LANES] = part.astype(BF16)
    peak[...] = after
    total[...] = total[...] * fade + gained
    flat = feats[...].reshape(rows * cols, chans)
    acc[...] = acc[...] * fade[:, :1] + jnp.dot(weight[...], flat, preferred_element_type=F32)

    @pl.when(step == pl.num_programs(0) - 1)
    def _():
        sub = meta[1]
        sums = acc[...].T
        tops = peak[...].T[:1]
        totals = jnp.sum(total[...].T, axis=0, keepdims=True)
        half = count // 2

        def write(ref, second):
            lanes = slice(half, count) if second else slice(0, half)
            ref[:chans, :] = sums[:, lanes]
            ref[chans : chans + 1, :] = tops[:, lanes]
            ref[chans + 1 : chans + 2, :] = totals[:, lanes]
            ref[chans + 2 :, :] = jnp.zeros((STATS - 2, half), F32)

        @pl.when(sub == 0)
        def _():
            write(keep, False)
            write(give, True)

        @pl.when(sub != 0)
        def _():
            write(keep, True)
            write(give, False)


def pool(meta, seeds, feats, protos):
    height, cols, chans = feats.shape
    count = protos.shape[0]
    rows = 8
    piece = jax.ShapeDtypeStruct((chans + STATS, count // 2), F32)
    whole = pl.BlockSpec((chans + STATS, count // 2), lambda i, *_: (0, 0))
    return pl.pallas_call(
        pool_kernel,
        out_shape=(piece, piece),
        grid_spec=pltpu.PrefetchScalarGridSpec(
            num_scalar_prefetch=1,
            grid=(height // rows,),
            in_specs=[
                pl.BlockSpec((rows, cols), lambda i, *_: (i, 0)),
                pl.BlockSpec((rows, cols, chans), lambda i, *_: (i, 0, 0)),
                pl.BlockSpec((count, chans), lambda i, *_: (0, 0)),
            ],
            out_specs=(whole, whole),
            scratch_shapes=[
                pltpu.VMEM((count, rows * cols), F32),
                pltpu.VMEM((count, rows * cols), BF16),
                pltpu.VMEM((count, chans), F32),
                pltpu.VMEM((count, LANES), F32),
                pltpu.VMEM((count, LANES), F32),
            ],
        ),
        compiler_params=pltpu.CompilerParams(vmem_limit_bytes=24 << 20),
        cost_estimate=cost(4 * height * cols * chans * count, height * cols * chans * 2),
        name="pool",
    )(meta, seeds, feats, protos)


def merge_kernel(a, b, out):
    chans = a.shape[0] - STATS
    at, bt = a[chans : chans + 1, :], b[chans : chans + 1, :]
    top = jnp.maximum(at, bt)
    fa, fb = jnp.exp(at - top), jnp.exp(bt - top)
    out[:chans, :] = a[:chans, :] * fa + b[:chans, :] * fb
    out[chans : chans + 1, :] = top
    out[chans + 1 : chans + 2, :] = (
        a[chans + 1 : chans + 2, :] * fa + b[chans + 1 : chans + 2, :] * fb
    )
    out[chans + 2 :, :] = jnp.zeros((STATS - 2, a.shape[1]), F32)


def merge(a, b):
    return pl.pallas_call(
        merge_kernel,
        out_shape=jax.ShapeDtypeStruct(a.shape, F32),
        in_specs=[VMEM, VMEM],
        out_specs=VMEM,
        compiler_params=params(2),
        cost_estimate=cost(3 * a.size, 12 * a.size),
        name="merge",
    )(a, b)


def field_kernel(meta, seeds, keep, got, near, far, *rest, sides):
    strips = rest[:sides]
    (
        taps, feats, refined, out,
        held, base, belief, second, lhs, lhs2, sums, mixed, sem, out_sem,
    ) = rest[sides:]
    height, cols, chans = feats.shape
    count = sums.shape[1]
    classes = count // 4
    sub, odd = meta[1], meta[2]
    groups = sem.shape[0]
    rows = height // groups

    def fetch(i):
        at = pl.ds(i * rows, rows)
        return pltpu.make_async_copy(feats.at[at], held.at[at], sem.at[i])

    for i in range(groups):
        fetch(i).start()

    half = count // 2
    first = pl.multiple_of(sub * half, half)
    other = pl.multiple_of((1 - sub) * half, half)
    sums[:, pl.ds(first, half)] = keep[...]
    sums[:, pl.ds(other, half)] = got[...]
    pooled = sums[:chans, :] / sums[chans + 1 : chans + 2, :]
    length = jnp.sqrt(jnp.sum(pooled * pooled, axis=0, keepdims=True) + 1e-06)
    ready = (pooled / length).T
    for c in range(chans // LANES):
        lanes = slice(c * LANES, (c + 1) * LANES)
        for m in range(4):
            mixed[c, pl.ds(m, classes, stride=4), :] = ready[m * classes : (m + 1) * classes, lanes]
        refined[:, lanes] = mixed[c]
    lead = (ready.astype(BF16).astype(F32) * SCALE).astype(BF16)

    labels = lax.broadcasted_iota(jnp.int32, (classes, 1), 0) + 1
    bonus = math.exp(SEED_REWARD)

    def share(grown):
        norm = jnp.sum(grown, axis=0, keepdims=True)
        return grown * (1.0 / jnp.maximum(norm, 1e-30))

    def unary(tokens, code):
        raw = lax.dot_general(lead, tokens, (((1,), (1,)), ((), ())), preferred_element_type=F32)
        parts = [raw[m * classes : (m + 1) * classes] for m in range(4)]
        top = functools.reduce(jnp.maximum, parts)
        top = jnp.max(top, axis=0, keepdims=True)
        top = jnp.where(code == 0, 1e30, top)
        grown = functools.reduce(jnp.add, [jnp.exp(part - top) for part in parts])
        grown = jnp.where(labels == code, grown * bonus, grown)
        return grown, share(grown)

    near_at = jnp.where(sub == 0, HALO + height, 0)
    far_at = jnp.where(sub == 0, 0, HALO + height)
    for i in range(HALO):
        for ref, at in ((near, near_at), (far, far_at)):
            tokens = ref[i * cols : (i + 1) * cols, :].astype(BF16)
            code = ref[HALO * cols + i : HALO * cols + i + 1, :].astype(jnp.int32)
            grown, early = unary(tokens, code)
            base[at + i, :, :cols] = grown
            belief[at + i, :, :cols] = early

    per = LANES // SIDE
    deep = height + 2 * HALO
    lane = lax.broadcasted_iota(jnp.int32, (classes, LANES), 1)
    for g in range(-(-deep // per)):
        found = []
        for strip in strips:
            tokens = strip[g * LANES : (g + 1) * LANES, :].astype(BF16)
            at = strip.shape[0] - STATS + g
            found.append(unary(tokens, strip[at : at + 1, :LANES].astype(jnp.int32)))
        for r in range(min(per, deep - g * per)):
            row = g * per + r
            for ref, one in ((base, 0), (belief, 1)):
                turn = (LANES - r * SIDE) % LANES
                value = pltpu.roll(found[0][one], turn, 1) if turn else found[0][one]
                if len(found) > 1:
                    turn = (turn + SIDE) % LANES
                    more = pltpu.roll(found[1][one], turn, 1) if turn else found[1][one]
                    value = jnp.where(lane < SIDE, value, more)
                ref[row, :, cols:] = value

    @pl.loop(0, groups)
    def _(i):
        fetch(i).wait()
        marks = jnp.where(meta[0] > 0, seeds[pl.ds(pl.multiple_of(i * rows, rows), rows), :] + 1, 0)
        for j in range(rows):
            row = i * rows + j
            grown, early = unary(held[row], marks[j : j + 1, :])
            base[HALO + row, :, :cols] = grown
            belief[HALO + row, :, :cols] = early

    def mix(source, start, batch, into):
        for k in range(0, classes, 16):
            for c in range(0, cols + LANES, LANES):
                cells = [
                    source[start - REACH + j, k : k + 16, c : c + LANES]
                    for j in range(batch + 2 * REACH)
                ]
                for j in range(batch):
                    tall = TAPS[0] * cells[j + REACH]
                    for d in range(1, REACH + 1):
                        tall = tall + TAPS[d] * (cells[j + REACH - d] + cells[j + REACH + d])
                    high = tall.astype(BF16)
                    low = (tall - high.astype(F32)).astype(BF16)
                    at = slice(j * classes + k, j * classes + k + 16)
                    if c < cols:
                        into[at, c : c + LANES] = high
                        into[at, cols + c : cols + c + LANES] = low
                    else:
                        into[at, 2 * cols : 2 * cols + LANES] = high
                        into[at, 2 * cols + LANES :] = low

    def spread(into, batch, width):
        return jnp.dot(
            into[: batch * classes, :], taps[odd, :, :width], preferred_element_type=F32
        )

    @pl.loop(0, (height + 2 * REACH) // 14)
    def _(i):
        start = REACH + i * 14
        for part, into in ((0, lhs), (7, lhs2)):
            mix(belief, start + part, 7, into)
        for part, into in ((0, lhs), (7, lhs2)):
            message = spread(into, 7, cols + LANES)
            for j in range(7):
                row = start + part + j
                sent = message[j * classes : (j + 1) * classes, :] - belief[row]
                second[row] = share(base[row] * jnp.exp(sent))

    def leave(row):
        return pltpu.make_async_copy(
            belief.at[row, :, pl.ds(0, cols)], out.at[:, row, :], out_sem.at[row]
        )

    @pl.loop(0, height // 8)
    def _(i):
        start = HALO + i * 8
        for part, into in ((0, lhs), (4, lhs2)):
            mix(second, start + part, 4, into)
        for part, into in ((0, lhs), (4, lhs2)):
            message = spread(into, 4, cols)
            for j in range(4):
                row = start + part + j
                sent = message[j * classes : (j + 1) * classes, :] - second[row, :, :cols]
                belief[row - HALO, :, :cols] = share(base[row, :, :cols] * jnp.exp(sent))
        for j in range(8):
            leave(i * 8 + j).start()

    @pl.loop(0, height)
    def _(i):
        leave(i).wait()


def field(meta, seeds, keep, got, near, far, strips, feats, count):
    height, cols, chans = feats.shape
    classes = count // 4
    wide = cols + LANES
    deep = height + 2 * HALO
    plane = pltpu.VMEM((deep, classes, wide), F32)
    return pl.pallas_call(
        functools.partial(field_kernel, sides=len(strips)),
        out_shape=(
            jax.ShapeDtypeStruct((count, chans), F32),
            jax.ShapeDtypeStruct((classes, height, cols), F32),
        ),
        in_specs=[SMEM] + [VMEM] * (6 + len(strips)) + [ANY],
        out_specs=(VMEM, ANY),
        scratch_shapes=[
            pltpu.VMEM((height, cols, chans), BF16),
            plane,
            plane,
            plane,
            pltpu.VMEM((8 * classes, 2 * wide), BF16),
            pltpu.VMEM((8 * classes, 2 * wide), BF16),
            pltpu.VMEM((chans + STATS, count), F32),
            pltpu.VMEM((chans // LANES, count, LANES), F32),
            pltpu.SemaphoreType.DMA((8,)),
            pltpu.SemaphoreType.DMA((height,)),
        ],
        compiler_params=params(44),
        cost_estimate=cost(8 * height * cols * chans * count, 16 << 20),
        name="field",
    )(meta, seeds, keep, got, near, far, *strips, jnp.asarray(across_taps(cols, len(strips)), BF16), feats)


def swap(x, axes, pairs):
    return lax.ppermute(x, axes, [p for a, b in pairs for p in ((a, b), (b, a))])


def on_device(features, seeds, valid_tiles, prototypes):
    height, cols, chans = features.shape
    classes, modes, _ = prototypes.shape
    count = classes * modes
    n_row, n_col = lax.axis_size("row"), lax.axis_size("col")
    sub, odd = lax.axis_index("sub"), lax.axis_index("col") % 2
    meta = jnp.stack([valid_tiles[0, 0], sub, odd]).astype(jnp.int32)
    protos = (SCALE * prototypes.astype(F32)).astype(BF16)
    protos = protos.transpose(1, 0, 2).reshape(count, chans)

    near, far = ends(meta, seeds, features)
    far = swap(far, ("row", "sub"), [(2 * i + 1, 2 * i + 2) for i in range(n_row - 1)])
    near = swap(near, "sub", [(0, 1)])

    keep, give = pool(meta, seeds, features, protos)
    keep = merge(keep, swap(give, "sub", [(0, 1)]))

    def doubled(keep, axis, size):
        stride = 1
        while stride < size:
            pairs = [(i, i | stride) for i in range(size) if not i & stride]
            keep = merge(keep, swap(keep, axis, pairs))
            stride *= 2
        return keep

    keep = doubled(keep, "col", n_col)
    keep, near, far = lax.optimization_barrier((keep, near, far))
    strips = [
        swap(
            side(meta, seeds, near, far, features),
            "col",
            [(i, i + 1) for i in range(0, n_col - 1, 2)],
        )
    ]
    if n_col > 2:
        other = jnp.stack([meta[0], meta[1], 1 - odd])
        strips.append(
            swap(
                side(other, seeds, near, far, features),
                "col",
                [(i, i + 1) for i in range(1, n_col - 1, 2)],
            )
        )
    keep = doubled(keep, "row", n_row)
    got = swap(keep, "sub", [(0, 1)])
    refined, belief = field(meta, seeds, keep, got, near, far, strips, features, count)
    return refined.reshape(classes, modes, chans), belief


def solution(mesh):
    placed = (
        P(("groups", "row", "sub"), "col", None),
        P(("groups", "row", "sub"), "col"),
        P(("groups", "row"), "col"),
        P("groups", None, None),
    )
    return jax.shard_map(
        on_device,
        mesh=mesh,
        in_specs=placed,
        out_specs=(P("groups", None, None), P("groups", ("row", "sub"), "col")),
        check_vma=False,
    )
```

```python
import functools
import math

import jax
import jax.numpy as jnp
import numpy as np
from jax import lax
from jax.experimental import pallas as pl
from jax.experimental.pallas import tpu as pltpu
from jax.sharding import PartitionSpec as P

ITERS = 2
SCALE = 2.0
SEED_REWARD = 2.0
LOW = -1e30
REACH = 3
HALO = ITERS * REACH
LANES = 128
STATS = 8
SIDE = 8
EDGE = 32
CHUNKS = 1
GAIN = 1.461325
TAPS = [math.exp(-(d * d) / 8.0) / GAIN for d in range(REACH + 1)]
F32 = jnp.float32
BF16 = jnp.bfloat16
VMEM = pl.BlockSpec(memory_space=pltpu.VMEM)
SMEM = pl.BlockSpec(memory_space=pltpu.SMEM)
ANY = pl.BlockSpec(memory_space=pl.ANY)
HBM = pl.BlockSpec(memory_space=pltpu.HBM)


def cost(flops, moved):
    return pl.CostEstimate(flops=flops, bytes_accessed=moved, transcendentals=0)


def params(mib):
    return pltpu.CompilerParams(vmem_limit_bytes=mib << 20)


def in_hbm(x):
    return pltpu.with_memory_space_constraint(x, pltpu.HBM)


def across_taps(cols, sides):
    nowhere = -(10**6)

    def stencil(source, target):
        gap = np.abs(source[:, None] - target[None, :])
        used = (source[:, None] != nowhere) & (target[None, :] != nowhere) & (gap <= REACH)
        return np.where(used, GAIN * np.exp(-np.minimum(gap, REACH) ** 2 / 8.0), 0.0)

    both = []
    for odd in (False, True):
        own = np.arange(cols)
        packed = np.full(LANES, nowhere)
        right, left = (EDGE + SIDE, EDGE) if odd else (EDGE, EDGE + SIDE)
        if sides == 2 or not odd:
            packed[right : right + HALO] = cols + np.arange(HALO)
        if sides == 2 or odd:
            packed[left + SIDE - HALO : left + SIDE] = np.arange(-HALO, 0)
        full = packed.copy()
        full[:EDGE] = own[:EDGE]
        full[LANES - EDGE :] = own[cols - EDGE :]
        main = stencil(own, own)
        near = stencil(packed, own)
        side = stencil(full, packed)
        none = np.zeros((cols, LANES))
        both.append(
            np.block([[main, none], [main, none], [near, side], [near, side]])
        )
    return np.stack(both)


def ends_kernel(meta, seeds, feats, near, far, held, labels, sem):
    height, cols, chans = feats.shape
    fetch = [
        pltpu.make_async_copy(feats.at[pl.ds(at, HALO)], held.at[i], sem.at[i])
        for i, at in enumerate((0, height - HALO))
    ] + [
        pltpu.make_async_copy(seeds.at[pl.ds(at, 8)], labels.at[i], sem.at[2 + i])
        for i, at in enumerate((0, height - 8))
    ]
    for copy in fetch:
        copy.start()
    for copy in fetch:
        copy.wait()

    def write(ref, i):
        at = (0, 8 - HALO)[i]
        for r in range(HALO):
            ref[r * cols : (r + 1) * cols, :] = held[i, r].astype(F32)
        marks = jnp.where(meta[0] > 0, labels[i, at : at + HALO, :] + 1, 0)
        ref[HALO * cols :, :] = marks.astype(F32)

    @pl.when(meta[1] == 0)
    def _():
        write(near, 1)
        write(far, 0)

    @pl.when(meta[1] != 0)
    def _():
        write(near, 0)
        write(far, 1)


def ends(meta, seeds, feats):
    height, cols, chans = feats.shape
    message = jax.ShapeDtypeStruct((HALO * cols + HALO, chans), F32)
    return pl.pallas_call(
        ends_kernel,
        out_shape=(message, message),
        in_specs=[SMEM, HBM, HBM],
        out_specs=(VMEM, VMEM),
        scratch_shapes=[
            pltpu.VMEM((2, HALO, cols, chans), BF16),
            pltpu.VMEM((2, 8, cols), jnp.int32),
            pltpu.SemaphoreType.DMA((4,)),
        ],
        compiler_params=params(8),
        cost_estimate=cost(0, 4 << 20),
        name="ends",
    )(meta, in_hbm(seeds), in_hbm(feats))


def side_kernel(meta, seeds, near, far, feats, out, marks):
    height, cols, chans = feats.shape
    deep = marks.shape[0]
    width = 2 * SIDE
    sub, left = meta[1], meta[2]
    marks[...] = jnp.zeros_like(marks)
    marks[HALO : HALO + height, :] = jnp.where(meta[0] > 0, seeds[...] + 1, 0).astype(F32)
    low, skip = HALO + height, jnp.where(left > 0, 0, cols - SIDE)
    skip = pl.multiple_of(skip, SIDE)

    def ends_of(ref, at):
        marks[at : at + HALO, :] = ref[HALO * cols :, :]
        for r in range(HALO):
            out[(at + r) * SIDE : (at + r + 1) * SIDE, :] = ref[pl.ds(r * cols + skip, SIDE), :]

    @pl.when(sub == 0)
    def _():
        ends_of(near, low)
        ends_of(far, 0)

    @pl.when(sub != 0)
    def _():
        ends_of(far, low)
        ends_of(near, 0)

    lane = lax.broadcasted_iota(jnp.int32, (cols, LANES), 1)
    source = lax.broadcasted_iota(jnp.int32, (cols, LANES), 0)
    spread = (source == lane % SIDE + skip).astype(BF16)
    spun = jnp.dot(marks[...].astype(BF16), spread, preferred_element_type=F32)
    per = LANES // SIDE
    groups = deep // per
    mine = lax.broadcasted_iota(jnp.int32, (per, LANES), 1) // SIDE
    mine = mine == lax.broadcasted_iota(jnp.int32, (per, LANES), 0)
    out[deep * SIDE :, :] = jnp.zeros((STATS, chans), F32)
    for g in range(groups):
        row = jnp.where(mine, spun[g * per : (g + 1) * per], 0.0)
        out[deep * SIDE + g : deep * SIDE + g + 1, :LANES] = jnp.sum(row, axis=0, keepdims=True)
    out[(height + 2 * HALO) * SIDE : deep * SIDE, :] = jnp.zeros(
        ((deep - height - 2 * HALO) * SIDE, chans), F32
    )

    @pl.when(left > 0)
    def _():
        for r in range(height):
            at = (HALO + r) * SIDE
            out[at : at + SIDE, :] = feats[r, :width].astype(F32)[:SIDE]

    @pl.when(left == 0)
    def _():
        for r in range(height):
            at = (HALO + r) * SIDE
            out[at : at + SIDE, :] = feats[r, cols - width :].astype(F32)[SIDE:]


def side(meta, seeds, near, far, feats):
    height, cols, chans = feats.shape
    per = LANES // SIDE
    deep = -(-(height + 2 * HALO) // per) * per
    return pl.pallas_call(
        side_kernel,
        out_shape=jax.ShapeDtypeStruct((deep * SIDE + STATS, chans), F32),
        in_specs=[SMEM, VMEM, VMEM, VMEM, VMEM],
        out_specs=VMEM,
        scratch_shapes=[pltpu.VMEM((deep, cols), F32)],
        compiler_params=params(8),
        cost_estimate=cost(0, 2 << 20),
        name="side",
    )(meta, seeds, near, far, feats)


def pool_kernel(meta, seeds, feats, given, *rest, rows):
    keep, give, scratch = rest[:CHUNKS], rest[CHUNKS : 2 * CHUNKS], rest[2 * CHUNKS :]
    score, weight, top = scratch[:2], scratch[2:4], scratch[4:6]
    acc, peak, total, protos = scratch[6:]
    height, cols, chans = feats.shape
    classes, modes, _ = given.shape
    count = classes * modes
    wide = given[...].astype(F32) * SCALE
    for m in range(modes):
        protos[m * classes : (m + 1) * classes, :] = wide[:, m, :].astype(BF16)
    chunks = height // rows
    acc[...] = jnp.zeros_like(acc)
    total[...] = jnp.zeros_like(total)
    peak[...] = jnp.full_like(peak, LOW)
    labels = lax.broadcasted_iota(jnp.int32, (classes, cols), 0)

    def rate(chunk, slot):
        best = jnp.full((count, LANES), LOW, F32)
        for r in range(rows):
            here = jnp.where(meta[0] > 0, seeds[pl.ds(chunk * rows + r, 1), :], -1)
            member = here == labels
            raw = lax.dot_general(
                protos[...],
                feats[chunk * rows + r],
                (((1,), (1,)), ((), ())),
                preferred_element_type=F32,
            )
            masked = jnp.concatenate(
                [
                    jnp.where(member, raw[m * classes : (m + 1) * classes], LOW)
                    for m in range(count // classes)
                ],
                axis=0,
            )
            score[slot][:, r * cols : (r + 1) * cols] = masked
            for c in range(cols // LANES):
                best = jnp.maximum(best, masked[:, c * LANES : (c + 1) * LANES])
        top[slot][...] = best

    def gather(chunk, slot):
        before = peak[...]
        after = jnp.maximum(before, jnp.max(top[slot][...], axis=1, keepdims=True))
        fade = jnp.exp(before - after)
        shift = jnp.maximum(after, 0.1 * LOW)
        gained = jnp.zeros((count, LANES), F32)
        for c in range(rows * cols // LANES):
            part = jnp.exp(score[slot][:, c * LANES : (c + 1) * LANES] - shift)
            gained = gained + part
            weight[slot][:, c * LANES : (c + 1) * LANES] = part.astype(BF16)
        peak[...] = after
        total[...] = total[...] * fade + gained
        flat = feats[pl.ds(chunk * rows, rows)].reshape(rows * cols, chans)
        grown = jnp.dot(weight[slot][...], flat, preferred_element_type=F32)
        for c in range(chans // LANES):
            lanes = slice(c * LANES, (c + 1) * LANES)
            acc[:, lanes] = acc[:, lanes] * fade + grown[:, lanes]

    rate(0, 0)

    @pl.loop(0, chunks // 2)
    def _(i):
        rate(2 * i + 1, 1)
        gather(2 * i, 0)
        rate(jnp.minimum(2 * i + 2, chunks - 1), 0)
        gather(2 * i + 1, 1)

    sub = meta[1]
    sums = acc[...].T
    tops = peak[...].T[:1]
    totals = jnp.sum(total[...].T, axis=0, keepdims=True)
    half = count // 2

    part = chans // CHUNKS

    def write(refs, second):
        lanes = slice(half, count) if second else slice(0, half)
        for i, ref in enumerate(refs):
            ref[:part, :] = sums[i * part : (i + 1) * part, lanes]
            ref[part : part + 1, :] = tops[:, lanes]
            ref[part + 1 : part + 2, :] = totals[:, lanes]
            ref[part + 2 :, :] = jnp.zeros((STATS - 2, half), F32)

    @pl.when(sub == 0)
    def _():
        write(keep, False)
        write(give, True)

    @pl.when(sub != 0)
    def _():
        write(keep, True)
        write(give, False)


def pool(meta, seeds, feats, protos):
    height, cols, chans = feats.shape
    count = protos.shape[0] * protos.shape[1]
    rows = 4
    piece = jax.ShapeDtypeStruct((chans // CHUNKS + STATS, count // 2), F32)
    flat = (count, rows * cols)
    narrow = pltpu.VMEM((count, LANES), F32)
    out = pl.pallas_call(
        functools.partial(pool_kernel, rows=rows),
        out_shape=(piece,) * (2 * CHUNKS),
        in_specs=[SMEM, VMEM, VMEM, VMEM],
        out_specs=(VMEM,) * (2 * CHUNKS),
        scratch_shapes=[pltpu.VMEM(flat, F32)] * 2
        + [pltpu.VMEM(flat, BF16)] * 2
        + [narrow] * 2
        + [pltpu.VMEM((count, chans), F32), narrow, narrow, pltpu.VMEM((count, chans), BF16)],
        compiler_params=params(8),
        cost_estimate=cost(4 * height * cols * chans * count, height * cols * chans * 2),
        name="pool",
    )(meta, seeds, feats, protos)
    return list(out[:CHUNKS]), list(out[CHUNKS:])


def merge_kernel(a, b, out):
    chans = a.shape[0] - STATS
    at, bt = a[chans : chans + 1, :], b[chans : chans + 1, :]
    top = jnp.maximum(at, bt)
    fa, fb = jnp.exp(at - top), jnp.exp(bt - top)
    out[:chans, :] = a[:chans, :] * fa + b[:chans, :] * fb
    out[chans : chans + 1, :] = top
    out[chans + 1 : chans + 2, :] = (
        a[chans + 1 : chans + 2, :] * fa + b[chans + 1 : chans + 2, :] * fb
    )
    out[chans + 2 :, :] = jnp.zeros((STATS - 2, a.shape[1]), F32)


def merge(a, b):
    return pl.pallas_call(
        merge_kernel,
        out_shape=jax.ShapeDtypeStruct(a.shape, F32),
        in_specs=[VMEM, VMEM],
        out_specs=VMEM,
        compiler_params=params(2),
        cost_estimate=cost(3 * a.size, 12 * a.size),
        name="merge",
    )(a, b)


def field_kernel(meta, seeds, *rest, sides):
    keep, got, near, far = rest[:CHUNKS], rest[CHUNKS : 2 * CHUNKS], *rest[2 * CHUNKS :][:2]
    rest = rest[2 * CHUNKS + 2 :]
    strips = rest[:sides]
    (
        taps, feats, refined, out,
        base, belief, second, lhs, lhs2, sums, result, out_sem,
    ) = rest[sides:]
    height, cols, chans = feats.shape
    count = sums.shape[1]
    classes = count // 4
    wide = cols + LANES
    sub, odd = meta[1], meta[2]
    half = count // 2
    first = pl.multiple_of(sub * half, half)
    other = pl.multiple_of((1 - sub) * half, half)
    part = chans // CHUNKS
    for refs, lanes in ((keep, pl.ds(first, half)), (got, pl.ds(other, half))):
        for i, ref in enumerate(refs):
            sums[i * part : (i + 1) * part, lanes] = ref[:part, :]
        sums[chans:, lanes] = ref[part:, :]
    pooled = sums[:chans, :] / sums[chans + 1 : chans + 2, :]
    length = jnp.sqrt(jnp.sum(pooled * pooled, axis=0, keepdims=True) + 1e-06)
    ready = (pooled / length).T
    for m in range(4):
        refined[:, m, :] = ready[m * classes : (m + 1) * classes, :]
    lead = (ready.astype(BF16).astype(F32) * SCALE).astype(BF16)

    labels = lax.broadcasted_iota(jnp.int32, (classes, 1), 0) + 1
    bonus = math.exp(SEED_REWARD)

    def share(grown):
        norm = jnp.sum(grown, axis=0, keepdims=True)
        return grown * (1.0 / jnp.maximum(norm, 1e-30))

    def unary(tokens, code):
        raw = lax.dot_general(lead, tokens, (((1,), (1,)), ((), ())), preferred_element_type=F32)
        parts = [raw[m * classes : (m + 1) * classes] for m in range(4)]
        top = functools.reduce(jnp.maximum, parts)
        top = jnp.max(top, axis=0, keepdims=True)
        top = jnp.where(code == 0, 1e30, top)
        grown = functools.reduce(jnp.add, [jnp.exp(part - top) for part in parts])
        grown = jnp.where(labels == code, grown * bonus, grown)
        return grown, share(grown)

    near_at = jnp.where(sub == 0, HALO + height, 0)
    far_at = jnp.where(sub == 0, 0, HALO + height)
    for i in range(HALO):
        for ref, at in ((near, near_at), (far, far_at)):
            tokens = ref[i * cols : (i + 1) * cols, :].astype(BF16)
            code = ref[HALO * cols + i : HALO * cols + i + 1, :].astype(jnp.int32)
            grown, early = unary(tokens, code)
            base[at + i, :, :cols] = grown
            belief[at + i, :, :cols] = early

    per = LANES // SIDE
    deep = height + 2 * HALO
    lane = lax.broadcasted_iota(jnp.int32, (classes, LANES), 1)
    for g in range(-(-deep // per)):
        found = []
        for strip in strips:
            tokens = strip[g * LANES : (g + 1) * LANES, :].astype(BF16)
            at = strip.shape[0] - STATS + g
            found.append(unary(tokens, strip[at : at + 1, :LANES].astype(jnp.int32)))
        for r in range(min(per, deep - g * per)):
            row = g * per + r
            for ref, one in ((base, 0), (belief, 1)):
                turn = (LANES + EDGE - r * SIDE) % LANES
                value = pltpu.roll(found[0][one], turn, 1) if turn else found[0][one]
                if len(found) > 1:
                    turn = (turn + SIDE) % LANES
                    more = pltpu.roll(found[1][one], turn, 1) if turn else found[1][one]
                    value = jnp.where(lane < EDGE + SIDE, value, more)
                ref[row, :, cols:] = value

    rows = 8

    @pl.loop(0, height // rows)
    def _(i):
        marks = jnp.where(meta[0] > 0, seeds[pl.ds(pl.multiple_of(i * rows, rows), rows), :] + 1, 0)
        for j in range(rows):
            row = i * rows + j
            grown, early = unary(feats[row], marks[j : j + 1, :])
            base[HALO + row, :, :cols] = grown
            belief[HALO + row, :, :cols] = early

    def mix(source, start, batch, into):
        for k in range(0, classes, 16):
            for c in range(0, cols + LANES, LANES):
                cells = [
                    source[start - REACH + j, k : k + 16, c : c + LANES]
                    for j in range(batch + 2 * REACH)
                ]
                for j in range(batch):
                    tall = TAPS[0] * cells[j + REACH]
                    for d in range(1, REACH + 1):
                        tall = tall + TAPS[d] * (cells[j + REACH - d] + cells[j + REACH + d])
                    high = tall.astype(BF16)
                    low = (tall - high.astype(F32)).astype(BF16)
                    at = slice(j * classes + k, j * classes + k + 16)
                    packed = 2 * cols
                    if c < cols:
                        into[at, c : c + LANES] = high
                        into[at, cols + c : cols + c + LANES] = low
                        keep = slice(0, 0)
                        if c == 0:
                            keep = slice(0, EDGE)
                        if c + LANES == cols:
                            keep = slice(LANES - EDGE, LANES)
                    else:
                        keep = slice(EDGE, LANES - EDGE)
                    if keep.stop:
                        for piece, place in ((high, packed), (low, packed + LANES)):
                            into[at, place + keep.start : place + keep.stop] = piece[:, keep]

    def sweep(source, start, stop, batch, settle):
        slots = (lhs, lhs2)

        @pl.loop(0, (stop - start) // (2 * batch))
        def _(i):
            for part, slot in enumerate(slots):
                mix(source, start + (2 * i + part) * batch, batch, slot)
            for part, slot in enumerate(slots):
                settle(2 * i + part, slot)

    def spread(slot, batch, rows, lanes):
        return jnp.dot(
            slot[: batch * classes, rows], taps[odd, rows, lanes], preferred_element_type=F32
        )

    def first(i, slot):
        main = spread(slot, 7, slice(0, 2 * wide), slice(0, cols))
        side = spread(slot, 7, slice(2 * cols, 2 * wide), slice(cols, wide))
        for j in range(7):
            row = REACH + i * 7 + j
            at = slice(j * classes, (j + 1) * classes)
            for got, lanes in ((main, slice(0, cols)), (side, slice(cols, wide))):
                sent = got[at, :] - belief[row, :, lanes]
                second[row, :, lanes] = share(base[row, :, lanes] * jnp.exp(sent))

    sweep(belief, REACH, height + HALO + REACH, 7, first)

    def leave(i):
        at = pl.ds(pl.multiple_of(i * 8, 8), 8)
        return pltpu.make_async_copy(result.at[:, at, :], out.at[:, at, :], out_sem.at[i])

    def last(i, slot):
        main = spread(slot, 8, slice(0, 2 * wide), slice(0, cols))
        for c in range(0, cols, LANES):
            lanes = slice(c, c + LANES)
            done = []
            for j in range(8):
                row = HALO + i * 8 + j
                sent = main[j * classes : (j + 1) * classes, lanes] - second[row, :, lanes]
                done.append(share(base[row, :, lanes] * jnp.exp(sent)))
            turned = jnp.transpose(jnp.stack(done), (1, 0, 2))
            result[:, pl.ds(pl.multiple_of(i * 8, 8), 8), lanes] = turned
        leave(i).start()

    sweep(second, HALO, HALO + height, 8, last)

    @pl.loop(0, height // 8)
    def _(i):
        leave(i).wait()


def field(meta, seeds, keep, got, near, far, strips, feats, count):
    height, cols, chans = feats.shape
    classes = count // 4
    wide = cols + LANES
    deep = height + 2 * HALO
    plane = pltpu.VMEM((deep, classes, wide), F32)
    return pl.pallas_call(
        functools.partial(field_kernel, sides=len(strips)),
        out_shape=(
            jax.ShapeDtypeStruct((classes, count // classes, chans), F32),
            jax.ShapeDtypeStruct((classes, height, cols), F32),
        ),
        in_specs=[SMEM] + [VMEM] * (5 + 2 * CHUNKS + len(strips)),
        out_specs=(VMEM, ANY),
        scratch_shapes=[
            plane,
            plane,
            plane,
            pltpu.VMEM((8 * classes, 2 * wide), BF16),
            pltpu.VMEM((8 * classes, 2 * wide), BF16),
            pltpu.VMEM((chans + STATS, count), F32),
            pltpu.VMEM((classes, height, cols), F32),
            pltpu.SemaphoreType.DMA((height // 8,)),
        ],
        compiler_params=params(38),
        cost_estimate=cost(8 * height * cols * chans * count, 16 << 20),
        name="field",
    )(meta, seeds, *keep, *got, near, far, *strips, jnp.asarray(across_taps(cols, len(strips)), BF16), feats)


def swap(x, axes, pairs):
    return lax.ppermute(x, axes, [p for a, b in pairs for p in ((a, b), (b, a))])


def on_device(features, seeds, valid_tiles, prototypes):
    height, cols, chans = features.shape
    classes, modes, _ = prototypes.shape
    count = classes * modes
    n_row, n_col = lax.axis_size("row"), lax.axis_size("col")
    sub, odd = lax.axis_index("sub"), lax.axis_index("col") % 2
    meta = jnp.stack([valid_tiles[0, 0], sub, odd]).astype(jnp.int32)

    near, far = ends(meta, seeds, features)
    far = swap(far, ("row", "sub"), [(2 * i + 1, 2 * i + 2) for i in range(n_row - 1)])
    near = swap(near, "sub", [(0, 1)])

    keep, give = pool(meta, seeds, features, prototypes)
    keep = [merge(k, swap(g, "sub", [(0, 1)])) for k, g in zip(keep, give)]

    near, far, _ = lax.optimization_barrier((near, far, keep))
    messages = [side(meta, seeds, near, far, features)]
    if n_col > 2:
        other = jnp.stack([meta[0], meta[1], 1 - odd])
        messages.append(side(other, seeds, near, far, features))

    def doubled(keep, axis, size, beside=()):
        stride = 1
        while stride < size:
            pairs = [(i, i | stride) for i in range(size) if not i & stride]
            got = [swap(k, axis, pairs) for k in keep]
            got, beside = lax.optimization_barrier((got, beside))
            keep = [merge(k, g) for k, g in zip(keep, got)]
            stride *= 2
        return keep, beside

    keep, messages = doubled(keep, "col", n_col, messages)
    messages, _ = lax.optimization_barrier((messages, keep))
    strips = [
        swap(message, "col", [(i, i + 1) for i in range(at, n_col - 1, 2)])
        for at, message in enumerate(messages)
    ]
    keep, _ = doubled(keep, "row", n_row)
    got = [swap(k, "sub", [(0, 1)]) for k in keep]
    refined, belief = field(meta, seeds, keep, got, near, far, strips, features, count)
    return refined, belief


def solution(mesh):
    placed = (
        P(("groups", "row", "sub"), "col", None),
        P(("groups", "row", "sub"), "col"),
        P(("groups", "row"), "col"),
        P("groups", None, None),
    )
    return jax.shard_map(
        on_device,
        mesh=mesh,
        in_specs=placed,
        out_specs=(P("groups", None, None), P("groups", ("row", "sub"), "col")),
        check_vma=False,
    )
```

```python
import functools
import math

import jax
import jax.numpy as jnp
import numpy as np
from jax import lax
from jax.experimental import pallas as pl
from jax.experimental.pallas import tpu as pltpu
from jax.sharding import PartitionSpec as P

ITERS = 2
SCALE = 2.0
SEED_REWARD = 2.0
LOW = -1e30
REACH = 3
HALO = ITERS * REACH
LANES = 128
STATS = 8
SIDE = 6
PER = LANES // SIDE
EDGE = 32
CHUNKS = 1
GAIN = 1.461325
TAPS = [math.exp(-(d * d) / 8.0) for d in range(REACH + 1)]
F32 = jnp.float32
BF16 = jnp.bfloat16
VMEM = pl.BlockSpec(memory_space=pltpu.VMEM)
SMEM = pl.BlockSpec(memory_space=pltpu.SMEM)
ANY = pl.BlockSpec(memory_space=pl.ANY)
HBM = pl.BlockSpec(memory_space=pltpu.HBM)


def cost(flops, moved):
    return pl.CostEstimate(flops=flops, bytes_accessed=moved, transcendentals=0)


def params(mib):
    return pltpu.CompilerParams(vmem_limit_bytes=mib << 20)


def in_hbm(x):
    return pltpu.with_memory_space_constraint(x, pltpu.HBM)


def across_taps(cols, sides):
    nowhere = -(10**6)

    def stencil(source, target):
        gap = np.abs(source[:, None] - target[None, :])
        used = (source[:, None] != nowhere) & (target[None, :] != nowhere) & (gap <= REACH)
        return np.where(used, GAIN * np.exp(-np.minimum(gap, REACH) ** 2 / 8.0), 0.0)

    both = []
    for odd in (False, True):
        own = np.arange(cols)
        packed = np.full(LANES, nowhere)
        right, left = (EDGE + SIDE, EDGE) if odd else (EDGE, EDGE + SIDE)
        if sides == 2 or not odd:
            packed[right : right + HALO] = cols + np.arange(HALO)
        if sides == 2 or odd:
            packed[left + SIDE - HALO : left + SIDE] = np.arange(-HALO, 0)
        full = packed.copy()
        full[:EDGE] = own[:EDGE]
        full[LANES - EDGE :] = own[cols - EDGE :]
        main = stencil(own, own)
        near = stencil(packed, own)
        side = stencil(full, packed)
        none = np.zeros((cols, LANES))
        both.append(
            np.block([[main, none], [main, none], [near, side], [near, side]])
        )
    return np.stack(both)


def ends_kernel(meta, seeds, feats, given, near, far, protos, held, labels, raw, sem):
    height, cols, chans = feats.shape
    classes, modes, _ = given.shape
    order = pltpu.make_async_copy(given, raw, sem.at[4])
    order.start()
    fetch = [
        pltpu.make_async_copy(feats.at[pl.ds(at, HALO)], held.at[i], sem.at[i])
        for i, at in enumerate((0, height - HALO))
    ] + [
        pltpu.make_async_copy(seeds.at[pl.ds(at, 8)], labels.at[i], sem.at[2 + i])
        for i, at in enumerate((0, height - 8))
    ]
    for copy in fetch:
        copy.start()
    order.wait()
    doubled = raw[...].astype(F32) * SCALE
    for m in range(modes):
        protos[m * classes : (m + 1) * classes, :] = doubled[:, m, :].astype(BF16)
    for copy in fetch:
        copy.wait()

    def write(ref, i):
        at = (0, 8 - HALO)[i]
        for r in range(HALO):
            ref[r * cols : (r + 1) * cols, :] = held[i, r].astype(F32)
        marks = jnp.where(meta[0] > 0, labels[i, at : at + HALO, :] + 1, 0)
        ref[HALO * cols :, :] = marks.astype(F32)

    @pl.when(meta[1] == 0)
    def _():
        write(near, 1)
        write(far, 0)

    @pl.when(meta[1] != 0)
    def _():
        write(near, 0)
        write(far, 1)


def ends(meta, seeds, feats, given):
    height, cols, chans = feats.shape
    classes, modes, _ = given.shape
    message = jax.ShapeDtypeStruct((HALO * cols + HALO, chans), F32)
    return pl.pallas_call(
        ends_kernel,
        out_shape=(message, message, jax.ShapeDtypeStruct((classes * modes, chans), BF16)),
        in_specs=[SMEM, HBM, HBM, HBM],
        out_specs=(VMEM, VMEM, VMEM),
        scratch_shapes=[
            pltpu.VMEM((2, HALO, cols, chans), BF16),
            pltpu.VMEM((2, 8, cols), jnp.int32),
            pltpu.VMEM(given.shape, BF16),
            pltpu.SemaphoreType.DMA((5,)),
        ],
        compiler_params=params(8),
        cost_estimate=cost(0, 4 << 20),
        name="ends",
    )(meta, in_hbm(seeds), in_hbm(feats), in_hbm(given))


def side_kernel(meta, seeds, near, far, feats, out, marks):
    height, cols, chans = feats.shape
    deep = marks.shape[0]
    width = 16
    sub, left = meta[1], meta[2]
    marks[...] = jnp.zeros_like(marks)
    marks[HALO : HALO + height, :] = jnp.where(meta[0] > 0, seeds[...] + 1, 0).astype(F32)
    low, skip = HALO + height, jnp.where(left > 0, 0, cols - SIDE)

    def place(row):
        at = row // PER * LANES + row % PER * SIDE
        return slice(at, at + SIDE)

    def ends_of(ref, at, last):
        marks[at : at + HALO, :] = ref[HALO * cols :, :]
        for r in range(HALO):
            first = (r + 1) * cols - SIDE if last else r * cols
            out[place(at + r), :] = ref[first : first + SIDE, :]

    def fill(last):
        @pl.when(sub == 0)
        def _():
            ends_of(near, low, last)
            ends_of(far, 0, last)

        @pl.when(sub != 0)
        def _():
            ends_of(far, low, last)
            ends_of(near, 0, last)

        for r in range(height):
            if last:
                rows = feats[r, cols - width :].astype(F32)[width - SIDE :]
            else:
                rows = feats[r, :width].astype(F32)[:SIDE]
            out[place(HALO + r), :] = rows

    groups = deep // PER
    out[groups * LANES :, :] = jnp.zeros((STATS, chans), F32)
    for g in range(groups):
        bare = max(0, min(PER, height + 2 * HALO - g * PER)) * SIDE
        out[g * LANES + bare : (g + 1) * LANES, :] = jnp.zeros((LANES - bare, chans), F32)

    @pl.when(left > 0)
    def _():
        fill(False)

    @pl.when(left == 0)
    def _():
        fill(True)

    lane = lax.broadcasted_iota(jnp.int32, (cols, LANES), 1)
    source = lax.broadcasted_iota(jnp.int32, (cols, LANES), 0)
    spread = (source == lane % SIDE + skip).astype(BF16)
    spun = jnp.dot(marks[...].astype(BF16), spread, preferred_element_type=F32)
    mine = lax.broadcasted_iota(jnp.int32, (PER, LANES), 1) // SIDE
    mine = mine == lax.broadcasted_iota(jnp.int32, (PER, LANES), 0)
    for g in range(groups):
        row = jnp.where(mine, spun[g * PER : (g + 1) * PER], 0.0)
        at = groups * LANES + g
        out[at : at + 1, :LANES] = jnp.sum(row, axis=0, keepdims=True)


def side(meta, seeds, near, far, feats):
    height, cols, chans = feats.shape
    deep = -(-(height + 2 * HALO) // PER) * PER
    return pl.pallas_call(
        side_kernel,
        out_shape=jax.ShapeDtypeStruct((deep // PER * LANES + STATS, chans), F32),
        in_specs=[SMEM, VMEM, VMEM, VMEM, VMEM],
        out_specs=VMEM,
        scratch_shapes=[pltpu.VMEM((deep, cols), F32)],
        compiler_params=params(8),
        cost_estimate=cost(0, 2 << 20),
        name="side",
    )(meta, seeds, near, far, feats)


def pool_kernel(meta, seeds, feats, protos, *rest, rows):
    keep, give, scratch = rest[:CHUNKS], rest[CHUNKS : 2 * CHUNKS], rest[2 * CHUNKS :]
    score, weight, top = scratch[:2], scratch[2:4], scratch[4:6]
    acc, peak, total = scratch[6:]
    height, cols, chans = feats.shape
    count = protos.shape[0]
    classes = count // 4
    chunks = height // rows
    acc[...] = jnp.zeros_like(acc)
    total[...] = jnp.zeros_like(total)
    peak[...] = jnp.full_like(peak, LOW)
    labels = lax.broadcasted_iota(jnp.int32, (classes, cols), 0)

    def rate(chunk, slot):
        best = jnp.full((count, LANES), LOW, F32)
        for r in range(rows):
            here = jnp.where(meta[0] > 0, seeds[pl.ds(chunk * rows + r, 1), :], -1)
            member = here == labels
            raw = lax.dot_general(
                protos[...],
                feats[chunk * rows + r],
                (((1,), (1,)), ((), ())),
                preferred_element_type=F32,
            )
            masked = jnp.concatenate(
                [
                    jnp.where(member, raw[m * classes : (m + 1) * classes], LOW)
                    for m in range(count // classes)
                ],
                axis=0,
            )
            score[slot][:, r * cols : (r + 1) * cols] = masked
            for c in range(cols // LANES):
                best = jnp.maximum(best, masked[:, c * LANES : (c + 1) * LANES])
        top[slot][...] = best

    def gather(chunk, slot):
        before = peak[...]
        after = jnp.maximum(before, jnp.max(top[slot][...], axis=1, keepdims=True))
        fade = jnp.exp(before - after)
        shift = jnp.maximum(after, 0.1 * LOW)
        gained = jnp.zeros((count, LANES), F32)
        for c in range(rows * cols // LANES):
            part = jnp.exp(score[slot][:, c * LANES : (c + 1) * LANES] - shift)
            gained = gained + part
            weight[slot][:, c * LANES : (c + 1) * LANES] = part.astype(BF16)
        peak[...] = after
        total[...] = total[...] * fade + gained
        flat = feats[pl.ds(chunk * rows, rows)].reshape(rows * cols, chans)
        grown = jnp.dot(weight[slot][...], flat, preferred_element_type=F32)
        for c in range(chans // LANES):
            lanes = slice(c * LANES, (c + 1) * LANES)
            acc[:, lanes] = acc[:, lanes] * fade + grown[:, lanes]

    rate(0, 0)

    @pl.loop(0, chunks // 2)
    def _(i):
        rate(2 * i + 1, 1)
        gather(2 * i, 0)
        rate(jnp.minimum(2 * i + 2, chunks - 1), 0)
        gather(2 * i + 1, 1)

    sub = meta[1]
    sums = acc[...].T
    tops = peak[...].T[:1]
    totals = jnp.sum(total[...].T, axis=0, keepdims=True)
    half = count // 2

    part = chans // CHUNKS

    def write(refs, second):
        lanes = slice(half, count) if second else slice(0, half)
        for i, ref in enumerate(refs):
            ref[:part, :] = sums[i * part : (i + 1) * part, lanes]
            ref[part : part + 1, :] = tops[:, lanes]
            ref[part + 1 : part + 2, :] = totals[:, lanes]
            ref[part + 2 :, :] = jnp.zeros((STATS - 2, half), F32)

    @pl.when(sub == 0)
    def _():
        write(keep, False)
        write(give, True)

    @pl.when(sub != 0)
    def _():
        write(keep, True)
        write(give, False)


def pool(meta, seeds, feats, protos):
    height, cols, chans = feats.shape
    count = protos.shape[0]
    rows = 16
    piece = jax.ShapeDtypeStruct((chans // CHUNKS + STATS, count // 2), F32)
    flat = (count, rows * cols)
    narrow = pltpu.VMEM((count, LANES), F32)
    out = pl.pallas_call(
        functools.partial(pool_kernel, rows=rows),
        out_shape=(piece,) * (2 * CHUNKS),
        in_specs=[SMEM, VMEM, VMEM, VMEM],
        out_specs=(VMEM,) * (2 * CHUNKS),
        scratch_shapes=[pltpu.VMEM(flat, F32)] * 2
        + [pltpu.VMEM(flat, BF16)] * 2
        + [narrow] * 2
        + [pltpu.VMEM((count, chans), F32), narrow, narrow],
        compiler_params=params(24),
        cost_estimate=cost(4 * height * cols * chans * count, height * cols * chans * 2),
        name="pool",
    )(meta, seeds, feats, protos)
    return list(out[:CHUNKS]), list(out[CHUNKS:])


def merge_kernel(a, b, out):
    chans = a.shape[0] - STATS
    at, bt = a[chans : chans + 1, :], b[chans : chans + 1, :]
    top = jnp.maximum(at, bt)
    fa, fb = jnp.exp(at - top), jnp.exp(bt - top)
    out[:chans, :] = a[:chans, :] * fa + b[:chans, :] * fb
    out[chans : chans + 1, :] = top
    out[chans + 1 : chans + 2, :] = (
        a[chans + 1 : chans + 2, :] * fa + b[chans + 1 : chans + 2, :] * fb
    )
    out[chans + 2 :, :] = jnp.zeros((STATS - 2, a.shape[1]), F32)


def merge(a, b):
    return pl.pallas_call(
        merge_kernel,
        out_shape=jax.ShapeDtypeStruct(a.shape, F32),
        in_specs=[VMEM, VMEM],
        out_specs=VMEM,
        compiler_params=params(2),
        cost_estimate=cost(3 * a.size, 12 * a.size),
        name="merge",
    )(a, b)


def field_kernel(meta, seeds, *rest, sides):
    keep, got, near, far = rest[:CHUNKS], rest[CHUNKS : 2 * CHUNKS], *rest[2 * CHUNKS :][:2]
    rest = rest[2 * CHUNKS + 2 :]
    strips = rest[:sides]
    (
        taps, feats, refined, out,
        base, belief, second, lhs, lhs2, sums, result, out_sem,
    ) = rest[sides:]
    height, cols, chans = feats.shape
    count = sums.shape[1]
    classes = count // 4
    wide = cols + LANES
    sub, odd = meta[1], meta[2]
    half = count // 2
    first = pl.multiple_of(sub * half, half)
    other = pl.multiple_of((1 - sub) * half, half)
    part = chans // CHUNKS
    for refs, lanes in ((keep, pl.ds(first, half)), (got, pl.ds(other, half))):
        for i, ref in enumerate(refs):
            sums[i * part : (i + 1) * part, lanes] = ref[:part, :]
        sums[chans:, lanes] = ref[part:, :]
    pooled = sums[:chans, :] / sums[chans + 1 : chans + 2, :]
    length = jnp.sqrt(jnp.sum(pooled * pooled, axis=0, keepdims=True) + 1e-06)
    ready = (pooled / length).T
    for m in range(4):
        refined[:, m, :] = ready[m * classes : (m + 1) * classes, :]
    lead = (ready.astype(BF16).astype(F32) * SCALE).astype(BF16)

    labels = lax.broadcasted_iota(jnp.int32, (classes, 1), 0) + 1
    bonus = math.exp(SEED_REWARD)

    def share(grown):
        norm = jnp.sum(grown, axis=0, keepdims=True)
        return grown * (1.0 / jnp.maximum(norm, 1e-30))

    def unary(tokens, code):
        raw = lax.dot_general(lead, tokens, (((1,), (1,)), ((), ())), preferred_element_type=F32)
        parts = [raw[m * classes : (m + 1) * classes] for m in range(4)]
        top = functools.reduce(jnp.maximum, parts)
        top = jnp.max(top, axis=0, keepdims=True)
        top = jnp.where(code == 0, 1e30, top)
        grown = functools.reduce(jnp.add, [jnp.exp(part - top) for part in parts])
        grown = jnp.where(labels == code, grown * bonus, grown)
        return grown, share(grown)

    near_at = jnp.where(sub == 0, HALO + height, 0)
    far_at = jnp.where(sub == 0, 0, HALO + height)
    for i in range(HALO):
        for ref, at in ((near, near_at), (far, far_at)):
            tokens = ref[i * cols : (i + 1) * cols, :].astype(BF16)
            code = ref[HALO * cols + i : HALO * cols + i + 1, :].astype(jnp.int32)
            grown, early = unary(tokens, code)
            base[at + i, :, :cols] = grown
            belief[at + i, :, :cols] = early

    per = PER
    deep = height + 2 * HALO
    lane = lax.broadcasted_iota(jnp.int32, (classes, LANES), 1)
    for g in range(-(-deep // per)):
        found = []
        for strip in strips:
            tokens = strip[g * LANES : (g + 1) * LANES, :].astype(BF16)
            at = strip.shape[0] - STATS + g
            found.append(unary(tokens, strip[at : at + 1, :LANES].astype(jnp.int32)))
        for r in range(min(per, deep - g * per)):
            row = g * per + r
            for ref, one in ((base, 0), (belief, 1)):
                turn = (LANES + EDGE - r * SIDE) % LANES
                value = pltpu.roll(found[0][one], turn, 1) if turn else found[0][one]
                if len(found) > 1:
                    turn = (turn + SIDE) % LANES
                    more = pltpu.roll(found[1][one], turn, 1) if turn else found[1][one]
                    value = jnp.where(lane < EDGE + SIDE, value, more)
                ref[row, :, cols:] = value

    rows = 16

    @pl.loop(0, height // rows)
    def _(i):
        marks = jnp.where(meta[0] > 0, seeds[pl.ds(pl.multiple_of(i * rows, rows), rows), :] + 1, 0)
        for j in range(rows):
            row = i * rows + j
            grown, early = unary(feats[row], marks[j : j + 1, :])
            base[HALO + row, :, :cols] = grown
            belief[HALO + row, :, :cols] = early

    def mix(source, start, batch, into):
        for k in range(0, classes, 16):
            for c in range(0, cols + LANES, LANES):
                cells = [
                    source[start - REACH + j, k : k + 16, c : c + LANES]
                    for j in range(batch + 2 * REACH)
                ]
                for j in range(batch):
                    tall = cells[j + REACH]
                    for d in range(1, REACH + 1):
                        tall = tall + TAPS[d] * (cells[j + REACH - d] + cells[j + REACH + d])
                    high = tall.astype(BF16)
                    low = (tall - high.astype(F32)).astype(BF16)
                    at = slice(j * classes + k, j * classes + k + 16)
                    packed = 2 * cols
                    if c < cols:
                        into[at, c : c + LANES] = high
                        into[at, cols + c : cols + c + LANES] = low
                        keep = slice(0, 0)
                        if c == 0:
                            keep = slice(0, EDGE)
                        if c + LANES == cols:
                            keep = slice(LANES - EDGE, LANES)
                    else:
                        keep = slice(EDGE, LANES - EDGE)
                    if keep.stop:
                        for piece, place in ((high, packed), (low, packed + LANES)):
                            into[at, place + keep.start : place + keep.stop] = piece[:, keep]

    def sweep(source, start, stop, batch, settle):
        slots = (lhs, lhs2)

        @pl.loop(0, (stop - start) // (2 * batch))
        def _(i):
            for part, slot in enumerate(slots):
                mix(source, start + (2 * i + part) * batch, batch, slot)
            for part, slot in enumerate(slots):
                settle(2 * i + part, slot)

    def spread(slot, batch, rows, lanes):
        return jnp.dot(
            slot[: batch * classes, rows], taps[odd, rows, lanes], preferred_element_type=F32
        )

    def first(i, slot):
        main = spread(slot, 7, slice(0, 2 * wide), slice(0, cols))
        side = spread(slot, 7, slice(2 * cols, 2 * wide), slice(cols, wide))
        for j in range(7):
            row = REACH + i * 7 + j
            at = slice(j * classes, (j + 1) * classes)
            for got, lanes in ((main, slice(0, cols)), (side, slice(cols, wide))):
                sent = got[at, :] * (1 / GAIN) - belief[row, :, lanes]
                second[row, :, lanes] = share(base[row, :, lanes] * jnp.exp(sent))

    sweep(belief, REACH, height + HALO + REACH, 7, first)

    def leave(i):
        at = pl.ds(pl.multiple_of(i * 8, 8), 8)
        return pltpu.make_async_copy(result.at[:, at, :], out.at[:, at, :], out_sem.at[i])

    def last(i, slot):
        main = spread(slot, 8, slice(0, 2 * wide), slice(0, cols))
        for c in range(0, cols, LANES):
            lanes = slice(c, c + LANES)
            done = []
            for j in range(8):
                row = HALO + i * 8 + j
                own = main[j * classes : (j + 1) * classes, lanes]
                sent = own * (1 / GAIN) - second[row, :, lanes]
                done.append(share(base[row, :, lanes] * jnp.exp(sent)))
            turned = jnp.transpose(jnp.stack(done), (1, 0, 2))
            result[:, pl.ds(pl.multiple_of(i * 8, 8), 8), lanes] = turned
        leave(i).start()

    sweep(second, HALO, HALO + height, 8, last)

    @pl.loop(0, height // 8)
    def _(i):
        leave(i).wait()


def field(meta, seeds, keep, got, near, far, strips, feats, count):
    height, cols, chans = feats.shape
    classes = count // 4
    wide = cols + LANES
    deep = height + 2 * HALO
    plane = pltpu.VMEM((deep, classes, wide), F32)
    return pl.pallas_call(
        functools.partial(field_kernel, sides=len(strips)),
        out_shape=(
            jax.ShapeDtypeStruct((classes, count // classes, chans), F32),
            jax.ShapeDtypeStruct((classes, height, cols), F32),
        ),
        in_specs=[SMEM] + [VMEM] * (5 + 2 * CHUNKS + len(strips)),
        out_specs=(VMEM, ANY),
        scratch_shapes=[
            plane,
            plane,
            plane,
            pltpu.VMEM((8 * classes, 2 * wide), BF16),
            pltpu.VMEM((8 * classes, 2 * wide), BF16),
            pltpu.VMEM((chans + STATS, count), F32),
            pltpu.VMEM((classes, height, cols), F32),
            pltpu.SemaphoreType.DMA((height // 8,)),
        ],
        compiler_params=params(38),
        cost_estimate=cost(8 * height * cols * chans * count, 16 << 20),
        name="field",
    )(meta, seeds, *keep, *got, near, far, *strips, jnp.asarray(across_taps(cols, len(strips)), BF16), feats)


def swap(x, axes, pairs):
    return lax.ppermute(x, axes, [p for a, b in pairs for p in ((a, b), (b, a))])


def on_device(features, seeds, valid_tiles, prototypes):
    height, cols, chans = features.shape
    classes, modes, _ = prototypes.shape
    count = classes * modes
    n_row, n_col = lax.axis_size("row"), lax.axis_size("col")
    sub, odd = lax.axis_index("sub"), lax.axis_index("col") % 2
    meta = jnp.stack([valid_tiles[0, 0], sub, odd]).astype(jnp.int32)

    near, far, protos = ends(meta, seeds, features, prototypes)
    far = swap(far, ("row", "sub"), [(2 * i + 1, 2 * i + 2) for i in range(n_row - 1)])
    near = swap(near, "sub", [(0, 1)])

    keep, give = pool(meta, seeds, features, protos)
    keep = [merge(k, swap(g, "sub", [(0, 1)])) for k, g in zip(keep, give)]

    def doubled(keep, axis, size, beside=()):
        stride = 1
        while stride < size:
            pairs = [(i, i | stride) for i in range(size) if not i & stride]
            got = [swap(k, axis, pairs) for k in keep]
            if stride == 1:
                got, beside = lax.optimization_barrier((got, beside))
            keep = [merge(k, g) for k, g in zip(keep, got)]
            stride *= 2
        return keep, beside

    keep, _ = doubled(keep, "col", n_col)
    near, far, _ = lax.optimization_barrier((near, far, keep))
    messages = [side(meta, seeds, near, far, features)]
    if n_col > 2:
        other = jnp.stack([meta[0], meta[1], 1 - odd])
        messages.append(side(other, seeds, near, far, features))
    keep, messages = doubled(keep, "row", n_row, messages)
    strips = [
        swap(message, "col", [(i, i + 1) for i in range(at, n_col - 1, 2)])
        for at, message in enumerate(messages)
    ]
    got = [swap(k, "sub", [(0, 1)]) for k in keep]
    refined, belief = field(meta, seeds, keep, got, near, far, strips, features, count)
    return refined, belief


def solution(mesh):
    placed = (
        P(("groups", "row", "sub"), "col", None),
        P(("groups", "row", "sub"), "col"),
        P(("groups", "row"), "col"),
        P("groups", None, None),
    )
    return jax.shard_map(
        on_device,
        mesh=mesh,
        in_specs=placed,
        out_specs=(P("groups", None, None), P("groups", ("row", "sub"), "col")),
        check_vma=False,
    )
```

```python
import functools
import math

import jax
import jax.numpy as jnp
import numpy as np
from jax import lax
from jax.experimental import pallas as pl
from jax.experimental.pallas import tpu as pltpu
from jax.sharding import PartitionSpec as P

ITERS = 2
SCALE = 2.0
SEED_REWARD = 2.0
LOW = -1e30
REACH = 3
HALO = ITERS * REACH
LANES = 128
STATS = 8
SIDE = 6
PER = LANES // SIDE
EDGE = 32
CHUNKS = 1
GAIN = 1.461325
TAPS = [math.exp(-(d * d) / 8.0) for d in range(REACH + 1)]
F32 = jnp.float32
BF16 = jnp.bfloat16
VMEM = pl.BlockSpec(memory_space=pltpu.VMEM)
SMEM = pl.BlockSpec(memory_space=pltpu.SMEM)
ANY = pl.BlockSpec(memory_space=pl.ANY)
HBM = pl.BlockSpec(memory_space=pltpu.HBM)


def cost(flops, moved):
    return pl.CostEstimate(flops=flops, bytes_accessed=moved, transcendentals=0)


def params(mib):
    return pltpu.CompilerParams(vmem_limit_bytes=mib << 20)


def in_hbm(x):
    return pltpu.with_memory_space_constraint(x, pltpu.HBM)


def across_taps(cols, sides):
    nowhere = -(10**6)

    def stencil(source, target):
        gap = np.abs(source[:, None] - target[None, :])
        used = (source[:, None] != nowhere) & (target[None, :] != nowhere) & (gap <= REACH)
        return np.where(used, GAIN * np.exp(-np.minimum(gap, REACH) ** 2 / 8.0), 0.0)

    both = []
    for odd in (False, True):
        own = np.arange(cols)
        packed = np.full(LANES, nowhere)
        right, left = (EDGE + SIDE, EDGE) if odd else (EDGE, EDGE + SIDE)
        if sides == 2 or not odd:
            packed[right : right + HALO] = cols + np.arange(HALO)
        if sides == 2 or odd:
            packed[left + SIDE - HALO : left + SIDE] = np.arange(-HALO, 0)
        full = packed.copy()
        full[:EDGE] = own[:EDGE]
        full[LANES - EDGE :] = own[cols - EDGE :]
        main = stencil(own, own)
        near = stencil(packed, own)
        side = stencil(full, packed)
        none = np.zeros((cols, LANES))
        both.append(
            np.block([[main, none], [main, none], [near, side], [near, side]])
        )
    return np.stack(both)


def ends_kernel(meta, seeds, feats, given, near, far, protos, held, labels, raw, sem):
    height, cols, chans = feats.shape
    classes, modes, _ = given.shape
    order = pltpu.make_async_copy(given, raw, sem.at[4])
    order.start()
    fetch = [
        pltpu.make_async_copy(feats.at[pl.ds(at, HALO)], held.at[i], sem.at[i])
        for i, at in enumerate((0, height - HALO))
    ] + [
        pltpu.make_async_copy(seeds.at[pl.ds(at, 8)], labels.at[i], sem.at[2 + i])
        for i, at in enumerate((0, height - 8))
    ]
    for copy in fetch:
        copy.start()
    order.wait()
    doubled = raw[...].astype(F32) * SCALE
    for m in range(modes):
        protos[m * classes : (m + 1) * classes, :] = doubled[:, m, :].astype(BF16)
    for copy in fetch:
        copy.wait()

    def write(ref, i):
        at = (0, 8 - HALO)[i]
        for r in range(HALO):
            ref[r * cols : (r + 1) * cols, :] = held[i, r].astype(F32)
        marks = jnp.where(meta[0] > 0, labels[i, at : at + HALO, :] + 1, 0)
        ref[HALO * cols :, :] = marks.astype(F32)

    @pl.when(meta[1] == 0)
    def _():
        write(near, 1)
        write(far, 0)

    @pl.when(meta[1] != 0)
    def _():
        write(near, 0)
        write(far, 1)


def ends(meta, seeds, feats, given):
    height, cols, chans = feats.shape
    classes, modes, _ = given.shape
    message = jax.ShapeDtypeStruct((HALO * cols + HALO, chans), F32)
    return pl.pallas_call(
        ends_kernel,
        out_shape=(message, message, jax.ShapeDtypeStruct((classes * modes, chans), BF16)),
        in_specs=[SMEM, HBM, HBM, HBM],
        out_specs=(VMEM, VMEM, VMEM),
        scratch_shapes=[
            pltpu.VMEM((2, HALO, cols, chans), BF16),
            pltpu.VMEM((2, 8, cols), jnp.int32),
            pltpu.VMEM(given.shape, BF16),
            pltpu.SemaphoreType.DMA((5,)),
        ],
        compiler_params=params(8),
        cost_estimate=cost(0, 4 << 20),
        name="ends",
    )(meta, in_hbm(seeds), in_hbm(feats), in_hbm(given))


def side_kernel(meta, seeds, near, far, feats, out, marks):
    height, cols, chans = feats.shape
    deep = marks.shape[0]
    width = 16
    sub, left = meta[1], meta[2]
    marks[...] = jnp.zeros_like(marks)
    marks[HALO : HALO + height, :] = jnp.where(meta[0] > 0, seeds[...] + 1, 0).astype(F32)
    low, skip = HALO + height, jnp.where(left > 0, 0, cols - SIDE)

    def place(row):
        at = row // PER * LANES + row % PER * SIDE
        return slice(at, at + SIDE)

    def ends_of(ref, at, last):
        marks[at : at + HALO, :] = ref[HALO * cols :, :]
        for r in range(HALO):
            first = (r + 1) * cols - SIDE if last else r * cols
            out[place(at + r), :] = ref[first : first + SIDE, :]

    def fill(last):
        @pl.when(sub == 0)
        def _():
            ends_of(near, low, last)
            ends_of(far, 0, last)

        @pl.when(sub != 0)
        def _():
            ends_of(far, low, last)
            ends_of(near, 0, last)

        for r in range(height):
            if last:
                rows = feats[r, cols - width :].astype(F32)[width - SIDE :]
            else:
                rows = feats[r, :width].astype(F32)[:SIDE]
            out[place(HALO + r), :] = rows

    groups = deep // PER
    out[groups * LANES :, :] = jnp.zeros((STATS, chans), F32)
    for g in range(groups):
        bare = max(0, min(PER, height + 2 * HALO - g * PER)) * SIDE
        out[g * LANES + bare : (g + 1) * LANES, :] = jnp.zeros((LANES - bare, chans), F32)

    @pl.when(left > 0)
    def _():
        fill(False)

    @pl.when(left == 0)
    def _():
        fill(True)

    lane = lax.broadcasted_iota(jnp.int32, (cols, LANES), 1)
    source = lax.broadcasted_iota(jnp.int32, (cols, LANES), 0)
    spread = (source == lane % SIDE + skip).astype(BF16)
    spun = jnp.dot(marks[...].astype(BF16), spread, preferred_element_type=F32)
    mine = lax.broadcasted_iota(jnp.int32, (PER, LANES), 1) // SIDE
    mine = mine == lax.broadcasted_iota(jnp.int32, (PER, LANES), 0)
    for g in range(groups):
        row = jnp.where(mine, spun[g * PER : (g + 1) * PER], 0.0)
        at = groups * LANES + g
        out[at : at + 1, :LANES] = jnp.sum(row, axis=0, keepdims=True)


def side(meta, seeds, near, far, feats):
    height, cols, chans = feats.shape
    deep = -(-(height + 2 * HALO) // PER) * PER
    return pl.pallas_call(
        side_kernel,
        out_shape=jax.ShapeDtypeStruct((deep // PER * LANES + STATS, chans), F32),
        in_specs=[SMEM, VMEM, VMEM, VMEM, VMEM],
        out_specs=VMEM,
        scratch_shapes=[pltpu.VMEM((deep, cols), F32)],
        compiler_params=params(8),
        cost_estimate=cost(0, 2 << 20),
        name="side",
    )(meta, seeds, near, far, feats)


def pool_kernel(meta, seeds, feats, protos, *rest, rows):
    keep, give, scratch = rest[:CHUNKS], rest[CHUNKS : 2 * CHUNKS], rest[2 * CHUNKS :]
    score, weight, top = scratch[:2], scratch[2:4], scratch[4:6]
    acc, peak, total = scratch[6:]
    height, cols, chans = feats.shape
    count = protos.shape[0]
    classes = count // 4
    chunks = height // rows
    acc[...] = jnp.zeros_like(acc)
    total[...] = jnp.zeros_like(total)
    peak[...] = jnp.full_like(peak, LOW)
    labels = lax.broadcasted_iota(jnp.int32, (classes, cols), 0)

    def rate(chunk, slot):
        best = jnp.full((count, LANES), LOW, F32)
        for r in range(rows):
            here = jnp.where(meta[0] > 0, seeds[pl.ds(chunk * rows + r, 1), :], -1)
            member = here == labels
            raw = lax.dot_general(
                protos[...],
                feats[chunk * rows + r],
                (((1,), (1,)), ((), ())),
                preferred_element_type=F32,
            )
            masked = jnp.concatenate(
                [
                    jnp.where(member, raw[m * classes : (m + 1) * classes], LOW)
                    for m in range(count // classes)
                ],
                axis=0,
            )
            score[slot][:, r * cols : (r + 1) * cols] = masked
            for c in range(cols // LANES):
                best = jnp.maximum(best, masked[:, c * LANES : (c + 1) * LANES])
        top[slot][...] = best

    def gather(chunk, slot):
        before = peak[...]
        after = jnp.maximum(before, jnp.max(top[slot][...], axis=1, keepdims=True))
        fade = jnp.exp(before - after)
        shift = jnp.maximum(after, 0.1 * LOW)
        gained = jnp.zeros((count, LANES), F32)
        for c in range(rows * cols // LANES):
            part = jnp.exp(score[slot][:, c * LANES : (c + 1) * LANES] - shift)
            gained = gained + part
            weight[slot][:, c * LANES : (c + 1) * LANES] = part.astype(BF16)
        peak[...] = after
        total[...] = total[...] * fade + gained
        flat = feats[pl.ds(chunk * rows, rows)].reshape(rows * cols, chans)
        grown = jnp.dot(weight[slot][...], flat, preferred_element_type=F32)
        for c in range(chans // LANES):
            lanes = slice(c * LANES, (c + 1) * LANES)
            acc[:, lanes] = acc[:, lanes] * fade + grown[:, lanes]

    rate(0, 0)

    @pl.loop(0, chunks // 2)
    def _(i):
        rate(2 * i + 1, 1)
        gather(2 * i, 0)
        rate(jnp.minimum(2 * i + 2, chunks - 1), 0)
        gather(2 * i + 1, 1)

    sub = meta[1]
    sums = acc[...].T
    tops = peak[...].T[:1]
    totals = jnp.sum(total[...].T, axis=0, keepdims=True)
    half = count // 2

    part = chans // CHUNKS

    def write(refs, second):
        lanes = slice(half, count) if second else slice(0, half)
        for i, ref in enumerate(refs):
            ref[:part, :] = sums[i * part : (i + 1) * part, lanes]
            ref[part : part + 1, :] = tops[:, lanes]
            ref[part + 1 : part + 2, :] = totals[:, lanes]
            ref[part + 2 :, :] = jnp.zeros((STATS - 2, half), F32)

    @pl.when(sub == 0)
    def _():
        write(keep, False)
        write(give, True)

    @pl.when(sub != 0)
    def _():
        write(keep, True)
        write(give, False)


def pool(meta, seeds, feats, protos):
    height, cols, chans = feats.shape
    count = protos.shape[0]
    rows = 16
    piece = jax.ShapeDtypeStruct((chans // CHUNKS + STATS, count // 2), F32)
    flat = (count, rows * cols)
    narrow = pltpu.VMEM((count, LANES), F32)
    out = pl.pallas_call(
        functools.partial(pool_kernel, rows=rows),
        out_shape=(piece,) * (2 * CHUNKS),
        in_specs=[SMEM, VMEM, VMEM, VMEM],
        out_specs=(VMEM,) * (2 * CHUNKS),
        scratch_shapes=[pltpu.VMEM(flat, F32)] * 2
        + [pltpu.VMEM(flat, BF16)] * 2
        + [narrow] * 2
        + [pltpu.VMEM((count, chans), F32), narrow, narrow],
        compiler_params=params(24),
        cost_estimate=cost(4 * height * cols * chans * count, height * cols * chans * 2),
        name="pool",
    )(meta, seeds, feats, protos)
    return list(out[:CHUNKS]), list(out[CHUNKS:])


def merge_kernel(a, b, out):
    chans = a.shape[0] - STATS
    at, bt = a[chans : chans + 1, :], b[chans : chans + 1, :]
    top = jnp.maximum(at, bt)
    fa, fb = jnp.exp(at - top), jnp.exp(bt - top)
    out[:chans, :] = a[:chans, :] * fa + b[:chans, :] * fb
    out[chans : chans + 1, :] = top
    out[chans + 1 : chans + 2, :] = (
        a[chans + 1 : chans + 2, :] * fa + b[chans + 1 : chans + 2, :] * fb
    )
    out[chans + 2 :, :] = jnp.zeros((STATS - 2, a.shape[1]), F32)


def merge(a, b):
    return pl.pallas_call(
        merge_kernel,
        out_shape=jax.ShapeDtypeStruct(a.shape, F32),
        in_specs=[VMEM, VMEM],
        out_specs=VMEM,
        compiler_params=params(2),
        cost_estimate=cost(3 * a.size, 12 * a.size),
        name="merge",
    )(a, b)


def field_kernel(meta, seeds, *rest, sides):
    keep, got, near, far = rest[:CHUNKS], rest[CHUNKS : 2 * CHUNKS], *rest[2 * CHUNKS :][:2]
    rest = rest[2 * CHUNKS + 2 :]
    strips = rest[:sides]
    (
        taps, feats, refined, out,
        base, belief, second, lhs, lhs2, sums, result, out_sem,
    ) = rest[sides:]
    height, cols, chans = feats.shape
    count = sums.shape[1]
    classes = count // 4
    wide = cols + LANES
    sub, odd = meta[1], meta[2]
    half = count // 2
    first = pl.multiple_of(sub * half, half)
    other = pl.multiple_of((1 - sub) * half, half)
    part = chans // CHUNKS
    for refs, lanes in ((keep, pl.ds(first, half)), (got, pl.ds(other, half))):
        for i, ref in enumerate(refs):
            sums[i * part : (i + 1) * part, lanes] = ref[:part, :]
        sums[chans:, lanes] = ref[part:, :]
    pooled = sums[:chans, :] / sums[chans + 1 : chans + 2, :]
    length = jnp.sqrt(jnp.sum(pooled * pooled, axis=0, keepdims=True) + 1e-06)
    ready = (pooled / length).T
    for m in range(4):
        refined[:, m, :] = ready[m * classes : (m + 1) * classes, :]
    lead = (ready.astype(BF16).astype(F32) * SCALE).astype(BF16)

    labels = lax.broadcasted_iota(jnp.int32, (classes, 1), 0) + 1
    bonus = math.exp(SEED_REWARD)

    def share(grown):
        norm = jnp.sum(grown, axis=0, keepdims=True)
        return grown * (1.0 / jnp.maximum(norm, 1e-30))

    def unary(tokens, code):
        raw = lax.dot_general(lead, tokens, (((1,), (1,)), ((), ())), preferred_element_type=F32)
        parts = [raw[m * classes : (m + 1) * classes] for m in range(4)]
        top = functools.reduce(jnp.maximum, parts)
        top = jnp.max(top, axis=0, keepdims=True)
        top = jnp.where(code == 0, 1e30, top)
        grown = functools.reduce(jnp.add, [jnp.exp(part - top) for part in parts])
        grown = jnp.where(labels == code, grown * bonus, grown)
        return grown, share(grown)

    near_at = jnp.where(sub == 0, HALO + height, 0)
    far_at = jnp.where(sub == 0, 0, HALO + height)
    for i in range(HALO):
        for ref, at in ((near, near_at), (far, far_at)):
            tokens = ref[i * cols : (i + 1) * cols, :].astype(BF16)
            code = ref[HALO * cols + i : HALO * cols + i + 1, :].astype(jnp.int32)
            grown, early = unary(tokens, code)
            base[at + i, :, :cols] = grown
            belief[at + i, :, :cols] = early

    per = PER
    deep = height + 2 * HALO
    lane = lax.broadcasted_iota(jnp.int32, (classes, LANES), 1)
    for g in range(-(-deep // per)):
        found = []
        for strip in strips:
            tokens = strip[g * LANES : (g + 1) * LANES, :].astype(BF16)
            at = strip.shape[0] - STATS + g
            found.append(unary(tokens, strip[at : at + 1, :LANES].astype(jnp.int32)))
        for r in range(min(per, deep - g * per)):
            row = g * per + r
            for ref, one in ((base, 0), (belief, 1)):
                turn = (LANES + EDGE - r * SIDE) % LANES
                value = pltpu.roll(found[0][one], turn, 1) if turn else found[0][one]
                if len(found) > 1:
                    turn = (turn + SIDE) % LANES
                    more = pltpu.roll(found[1][one], turn, 1) if turn else found[1][one]
                    value = jnp.where(lane < EDGE + SIDE, value, more)
                ref[row, :, cols:] = value

    rows = 32

    @pl.loop(0, height // rows)
    def _(i):
        marks = jnp.where(meta[0] > 0, seeds[pl.ds(pl.multiple_of(i * rows, rows), rows), :] + 1, 0)
        for j in range(rows):
            row = i * rows + j
            grown, early = unary(feats[row], marks[j : j + 1, :])
            base[HALO + row, :, :cols] = grown
            belief[HALO + row, :, :cols] = early

    def mix(source, start, batch, into):
        for k in range(0, classes, 16):
            for c in range(0, cols + LANES, LANES):
                cells = [
                    source[start - REACH + j, k : k + 16, c : c + LANES]
                    for j in range(batch + 2 * REACH)
                ]
                for j in range(batch):
                    tall = cells[j + REACH]
                    for d in range(1, REACH + 1):
                        tall = tall + TAPS[d] * (cells[j + REACH - d] + cells[j + REACH + d])
                    high = tall.astype(BF16)
                    low = (tall - high.astype(F32)).astype(BF16)
                    at = slice(j * classes + k, j * classes + k + 16)
                    packed = 2 * cols
                    if c < cols:
                        into[at, c : c + LANES] = high
                        into[at, cols + c : cols + c + LANES] = low
                        keep = slice(0, 0)
                        if c == 0:
                            keep = slice(0, EDGE)
                        if c + LANES == cols:
                            keep = slice(LANES - EDGE, LANES)
                    else:
                        keep = slice(EDGE, LANES - EDGE)
                    if keep.stop:
                        for piece, place in ((high, packed), (low, packed + LANES)):
                            into[at, place + keep.start : place + keep.stop] = piece[:, keep]

    def sweep(source, start, stop, batch, settle):
        slots = (lhs, lhs2)

        @pl.loop(0, (stop - start) // (2 * batch))
        def _(i):
            for part, slot in enumerate(slots):
                mix(source, start + (2 * i + part) * batch, batch, slot)
            for part, slot in enumerate(slots):
                settle(2 * i + part, slot)

    def spread(slot, batch, rows, lanes):
        return jnp.dot(
            slot[: batch * classes, rows], taps[odd, rows, lanes], preferred_element_type=F32
        )

    def first(i, slot):
        main = spread(slot, 7, slice(0, 2 * wide), slice(0, cols))
        side = spread(slot, 7, slice(2 * cols, 2 * wide), slice(cols, wide))
        for j in range(7):
            row = REACH + i * 7 + j
            at = slice(j * classes, (j + 1) * classes)
            for got, lanes in ((main, slice(0, cols)), (side, slice(cols, wide))):
                sent = got[at, :] * (1 / GAIN) - belief[row, :, lanes]
                second[row, :, lanes] = share(base[row, :, lanes] * jnp.exp(sent))

    sweep(belief, REACH, height + HALO + REACH, 7, first)

    def leave(i):
        at = pl.ds(pl.multiple_of(i * 8, 8), 8)
        return pltpu.make_async_copy(result.at[:, at, :], out.at[:, at, :], out_sem.at[i])

    def last(i, slot):
        main = spread(slot, 8, slice(0, 2 * wide), slice(0, cols))
        for c in range(0, cols, LANES):
            lanes = slice(c, c + LANES)
            done = []
            for j in range(8):
                row = HALO + i * 8 + j
                own = main[j * classes : (j + 1) * classes, lanes]
                sent = own * (1 / GAIN) - second[row, :, lanes]
                done.append(share(base[row, :, lanes] * jnp.exp(sent)))
            turned = jnp.transpose(jnp.stack(done), (1, 0, 2))
            result[:, pl.ds(pl.multiple_of(i * 8, 8), 8), lanes] = turned
        leave(i).start()

    sweep(second, HALO, HALO + height, 8, last)

    @pl.loop(0, height // 8)
    def _(i):
        leave(i).wait()


def field(meta, seeds, keep, got, near, far, strips, feats, count):
    height, cols, chans = feats.shape
    classes = count // 4
    wide = cols + LANES
    deep = height + 2 * HALO
    plane = pltpu.VMEM((deep, classes, wide), F32)
    return pl.pallas_call(
        functools.partial(field_kernel, sides=len(strips)),
        out_shape=(
            jax.ShapeDtypeStruct((classes, count // classes, chans), F32),
            jax.ShapeDtypeStruct((classes, height, cols), F32),
        ),
        in_specs=[SMEM] + [VMEM] * (5 + 2 * CHUNKS + len(strips)),
        out_specs=(VMEM, ANY),
        scratch_shapes=[
            plane,
            plane,
            plane,
            pltpu.VMEM((8 * classes, 2 * wide), BF16),
            pltpu.VMEM((8 * classes, 2 * wide), BF16),
            pltpu.VMEM((chans + STATS, count), F32),
            pltpu.VMEM((classes, height, cols), F32),
            pltpu.SemaphoreType.DMA((height // 8,)),
        ],
        compiler_params=params(38),
        cost_estimate=cost(8 * height * cols * chans * count, 16 << 20),
        name="field",
    )(meta, seeds, *keep, *got, near, far, *strips, jnp.asarray(across_taps(cols, len(strips)), BF16), feats)


def swap(x, axes, pairs):
    return lax.ppermute(x, axes, [p for a, b in pairs for p in ((a, b), (b, a))])


def on_device(features, seeds, valid_tiles, prototypes):
    height, cols, chans = features.shape
    classes, modes, _ = prototypes.shape
    count = classes * modes
    n_row, n_col = lax.axis_size("row"), lax.axis_size("col")
    sub, odd = lax.axis_index("sub"), lax.axis_index("col") % 2
    meta = jnp.stack([valid_tiles[0, 0], sub, odd]).astype(jnp.int32)

    near, far, protos = ends(meta, seeds, features, prototypes)
    far = swap(far, ("row", "sub"), [(2 * i + 1, 2 * i + 2) for i in range(n_row - 1)])
    near = swap(near, "sub", [(0, 1)])

    keep, give = pool(meta, seeds, features, protos)
    keep = [merge(k, swap(g, "sub", [(0, 1)])) for k, g in zip(keep, give)]

    def doubled(keep, axis, size, beside=()):
        stride = 1
        while stride < size:
            pairs = [(i, i | stride) for i in range(size) if not i & stride]
            got = [swap(k, axis, pairs) for k in keep]
            if stride == 1:
                got, beside = lax.optimization_barrier((got, beside))
            keep = [merge(k, g) for k, g in zip(keep, got)]
            stride *= 2
        return keep, beside

    keep, _ = doubled(keep, "col", n_col)
    near, far, _ = lax.optimization_barrier((near, far, keep))
    messages = [side(meta, seeds, near, far, features)]
    if n_col > 2:
        other = jnp.stack([meta[0], meta[1], 1 - odd])
        messages.append(side(other, seeds, near, far, features))
    keep, messages = doubled(keep, "row", n_row, messages)
    strips = [
        swap(message, "col", [(i, i + 1) for i in range(at, n_col - 1, 2)])
        for at, message in enumerate(messages)
    ]
    got = [swap(k, "sub", [(0, 1)]) for k in keep]
    refined, belief = field(meta, seeds, keep, got, near, far, strips, features, count)
    return refined, belief


def solution(mesh):
    placed = (
        P(("groups", "row", "sub"), "col", None),
        P(("groups", "row", "sub"), "col"),
        P(("groups", "row"), "col"),
        P("groups", None, None),
    )
    return jax.shard_map(
        on_device,
        mesh=mesh,
        in_specs=placed,
        out_specs=(P("groups", None, None), P("groups", ("row", "sub"), "col")),
        check_vma=False,
    )
```
